128 devices in a mesh: row: 8 (over x, core), col: 16 (over z, y).
Axes of the slice: x: 4, y: 4, z: 4, core: 2. Of those that a mesh axis runs over, the one named last changes fastest.
Arguments:
- counts: float32 [8192, 8192], P('row', 'col'), may hold values from 0 to 514, as said below
- labels: int32 [983040], replicated, may hold values from 0 to 8191, as said below
- edge_tiles: int32 [4096, 2, 128], P(('row', 'col')), may hold values from 0 to 983039, as said below
- proposals: int32 [2, 256], replicated, may hold values from 0 to 8191, as said below
- accept_flags: int32 [256], P('col'), may hold values 0 or 1
Outputs:
- count_matrix: float32 [8192, 8192], P('row', 'col')
- merge_cost: float32 [256], P('col')
- accepted_cost: float32 [256], P('col')
The draws below stay inside these ranges and needn't reach their ends.
Inputs may be any that keep to these rules, and one draw needn't show every extreme that they name: `counts`: Symmetric, whole numbers, every diagonal entry at least 2. `labels`: every block holds exactly 120 vertices. `edge_tiles`: each edge gives the two entries (label of its first vertex, label of its second) and the reverse; entry (r, s) lies in tile (r // 1024, s // 512). Of the 8192 entries of one device's edges at most 144 lie in one tile, and in every draw some tile gets exactly 144 entries from every device. proposals[1, p] differs from proposals[0, p]; for p // 16 = c, proposals[0, p] lies in c * 512 to (c + 1) * 512 - 1, and these sources are distinct.
All inputs are finite; a program needn't handle non-finite values. No bound on the sum of `accept_flags` on one device may be relied on, other than what follows from the above.
Results may differ from the reference program's by a relative error of at most 0.0003.
Values sent between devices are 32-bit elements; how exact they have to be, the bound alone decides.
A program may use at most 128 MiB of HBM per device.

```python
import jax
import jax.numpy as jnp

BLOCKS = 8192
VPB = 120
E_DEV = 4096
PROP_COL = 16
SENDERS = 128
ROWS_TILE = 1024
COLS_TILE = 512
CAP = 144
VERTICES = 983040
EDGE_TILES = 4096
PROPOSALS = 256


def vertex_order(key):
    return jax.random.permutation(jax.random.fold_in(key, 11), VERTICES).astype(jnp.int32)


def draw_counts(key, part):
    count_key = jax.random.fold_in(key, 31)
    first_key, second_key = jax.random.split(count_key)
    upper_level = 9
    activity = jax.random.randint(first_key, (BLOCKS,), 1, upper_level, dtype=jnp.int32)
    widths = activity[:, None] * activity[None, :]
    upper = jax.random.randint(second_key, (BLOCKS, BLOCKS), 0, 1 + widths, dtype=jnp.int32)
    diagonal = 2 * jnp.eye(BLOCKS, dtype=jnp.int32)
    return (upper + upper.T + diagonal).astype(jnp.float32)


def draw_labels(key, part):
    order = vertex_order(key)
    inverse = jnp.argsort(order, stable=True).astype(jnp.int32)
    return (inverse % BLOCKS).astype(jnp.int32)


def draw_edge_tiles(key, part):
    order = vertex_order(key)
    edge_key = jax.random.fold_in(key, 23)
    row_tiles = BLOCKS // ROWS_TILE
    col_tiles = BLOCKS // COLS_TILE
    tile_count = row_tiles * col_tiles
    per_tile = CAP // 3
    slot_count = tile_count * per_tile
    hot_row = jax.random.randint(jax.random.fold_in(edge_key, 1), (), 0, row_tiles, dtype=jnp.int32)
    hot_col = (2 * hot_row + 2 + jax.random.randint(jax.random.fold_in(edge_key, 2), (), 0, col_tiles - 2, dtype=jnp.int32)) % col_tiles
    hot_tile = hot_row * col_tiles + hot_col
    first_pre = hot_col // 2 * col_tiles + 2 * hot_row
    second_pre = first_pre + 1
    half_bit = hot_col % 2
    offsets = jax.random.randint(jax.random.fold_in(edge_key, 3), (tile_count,), 0, 65536, dtype=jnp.int32)
    device_keys = jax.random.split(jax.random.fold_in(edge_key, 4), SENDERS)

    def one_device(device_key):
        keys = jax.random.split(device_key, 7)
        slots = jnp.arange(slot_count, dtype=jnp.int32)
        slot_tile = slots // per_tile
        noise = jax.random.randint(keys[0], (slot_count,), 0, 65536, dtype=jnp.int32)
        score = (noise + offsets[slot_tile]) * slot_count + slots
        forced = (slot_tile == hot_tile) | (slot_tile == first_pre) | (slot_tile == second_pre)
        score = jnp.where(forced, score - 2 ** 30, score)
        chosen = jnp.argsort(score, stable=True)[:E_DEV]
        tiles = slot_tile[chosen]
        tile_row = tiles // col_tiles
        tile_col = tiles % col_tiles
        pre_tile = (tiles == first_pre) | (tiles == second_pre)
        free_row = tile_row * ROWS_TILE + jax.random.randint(keys[1], (E_DEV,), 0, ROWS_TILE, dtype=jnp.int32)
        bound_row = tile_row * ROWS_TILE + half_bit * COLS_TILE + jax.random.randint(keys[2], (E_DEV,), 0, COLS_TILE, dtype=jnp.int32)
        row_block = jnp.where(pre_tile, bound_row, free_row)
        col_block = tile_col * COLS_TILE + jax.random.randint(keys[3], (E_DEV,), 0, COLS_TILE, dtype=jnp.int32)
        first_member = jax.random.randint(keys[4], (E_DEV,), 0, VPB, dtype=jnp.int32)
        second_member = jax.random.randint(keys[5], (E_DEV,), 0, VPB, dtype=jnp.int32)
        first_vertex = order[row_block + BLOCKS * first_member]
        second_vertex = order[col_block + BLOCKS * second_member]
        shuffle = jax.random.permutation(keys[6], E_DEV)
        first_vertex = first_vertex[shuffle].reshape(E_DEV // 128, 128)
        second_vertex = second_vertex[shuffle].reshape(E_DEV // 128, 128)
        return jnp.stack([first_vertex, second_vertex], axis=1)
    stacked = jax.vmap(one_device)(device_keys)
    return stacked.reshape(EDGE_TILES, 2, 128).astype(jnp.int32)


def draw_proposals(key, part):
    proposal_key = jax.random.fold_in(key, 41)
    groups = PROPOSALS // PROP_COL
    group_keys = jax.random.split(proposal_key, groups)

    def one_group(group_key, group_index):
        first_key, second_key = jax.random.split(group_key)
        picks = jax.random.permutation(first_key, COLS_TILE)[:PROP_COL].astype(jnp.int32)
        source = group_index * COLS_TILE + picks
        target = (source + 1 + jax.random.randint(second_key, (PROP_COL,), 0, BLOCKS - 1, dtype=jnp.int32)) % BLOCKS
        return (source, target)
    sources, targets = jax.vmap(one_group)(group_keys, jnp.arange(groups, dtype=jnp.int32))
    return jnp.stack([sources.reshape(-1), targets.reshape(-1)]).astype(jnp.int32)


def touch_ends(entries, key, least, largest):
    dims = entries.shape
    index_at = [jax.random.randint(jax.random.fold_in(key, axis), (), 0, dims[axis]) for axis in range(len(dims))]
    entries = entries.at[tuple(index_at)].set(least)
    longest = dims.index(max(dims))
    index_at[longest] = (index_at[longest] + 1) % dims[longest]
    return entries.at[tuple(index_at)].set(largest)


def setup_inputs(seed: int = 0) -> dict:
    key_list = jax.random.split(jax.random.key(seed), 6)
    return {
        "counts": draw_counts(jax.random.fold_in(key_list[5], 71), 0),
        "labels": draw_labels(jax.random.fold_in(key_list[5], 71), 0),
        "edge_tiles": draw_edge_tiles(jax.random.fold_in(key_list[5], 71), 0),
        "proposals": draw_proposals(jax.random.fold_in(key_list[5], 71), 0),
        "accept_flags": touch_ends((jax.random.randint(key_list[4], (PROPOSALS,), 0, 2) < 1).astype(jnp.int32), jax.random.fold_in(key_list[4], 1), 0, 1),
    }


def entropy_term(value):
    return value * jnp.log(jnp.maximum(value, 1.0))


def reference(counts, labels, edge_tiles, proposals, accept_flags):
    first_label = labels[edge_tiles[:, 0, :].reshape(-1)]
    second_label = labels[edge_tiles[:, 1, :].reshape(-1)]
    increments = jnp.zeros((BLOCKS, BLOCKS), jnp.float32).at[first_label, second_label].add(jnp.float32(1.0))
    count_matrix = counts + increments + increments.T
    source = proposals[0]
    target = proposals[1]
    own_row = count_matrix[source]
    other_row = count_matrix[target]
    positions = jnp.arange(BLOCKS, dtype=jnp.int32)
    at_source = positions[None, :] == source[:, None]
    at_target = positions[None, :] == target[:, None]
    mixed = entropy_term(own_row + other_row) - entropy_term(own_row) - entropy_term(other_row)
    pair_sum = jnp.sum(jnp.where(at_source | at_target, jnp.float32(0.0), mixed), axis=1)
    self_source = jnp.sum(jnp.where(at_source, own_row, jnp.float32(0.0)), axis=1)
    cross_count = jnp.sum(jnp.where(at_source, other_row, jnp.float32(0.0)), axis=1)
    self_target = jnp.sum(jnp.where(at_target, other_row, jnp.float32(0.0)), axis=1)
    degree_source = jnp.sum(own_row, axis=1)
    degree_target = jnp.sum(other_row, axis=1)
    corner = entropy_term(self_source + 2.0 * cross_count + self_target) - entropy_term(self_source) - entropy_term(self_target) - 2.0 * entropy_term(cross_count)
    change = -(pair_sum + 0.5 * corner) + entropy_term(degree_source + degree_target) - entropy_term(degree_source) - entropy_term(degree_target)
    merge_cost = change / BLOCKS
    accepted_cost = jnp.where(accept_flags == 1, merge_cost, jnp.float32(0.0))
    return count_matrix, merge_cost, accepted_cost
```

```python
import functools

import jax
import jax.numpy as jnp
from jax import lax
from jax.experimental import pallas as pl
from jax.experimental.pallas import tpu as pltpu
from jax.sharding import PartitionSpec as P

I32 = jnp.int32
F32 = jnp.float32
BF = jnp.bfloat16
F8 = jnp.float8_e4m3fn
LANES = 128
BLOCKS = 8192
PROP_COL = 16
MESH = pl.DeviceIdType.MESH


def start_gather(evm, hi, sms, sem):
    hi[...] = lax.shift_right_logical(evm[...], 7)
    for k in range(len(sms)):
        pltpu.make_async_copy(hi.at[k], sms[k], sem.at[k]).start()


def gather_labels(evm, table, lab, hi, sms, g, sem):
    tiles = evm.shape[0]
    depth = len(sms)
    sub = lax.broadcasted_iota(I32, (LANES, LANES), 0)

    def finish(t, slot):
        for side in (0, 1):
            lanes = evm[t, pl.ds(side, 1), :] & (LANES - 1)
            picked = jnp.where(sub == lanes, g[slot, side].T, 0)
            lab[pl.ds(side, 1), pl.ds(pl.multiple_of(t * LANES, LANES), LANES)] = jnp.sum(
                picked, axis=0, keepdims=True
            )

    def body(u, _):
        for k in range(depth):
            t = depth * u + k
            pltpu.make_async_copy(hi.at[t], sms[k], sem.at[k]).wait()
            finish(jnp.maximum(t - 1, 0), (k + 1) % 2)
            for side in (0, 1):
                for e in range(LANES):
                    g[k % 2, side, pl.ds(e, 1), :] = table[pl.ds(sms[k][side, e], 1), :]
            later = jnp.minimum(t + depth, tiles - 1)
            pltpu.make_async_copy(hi.at[later], sms[k], sem.at[k]).start()
        return 0

    lax.fori_loop(0, tiles // depth, body, 0)
    for k in range(depth):
        pltpu.make_async_copy(hi.at[tiles - 1], sms[k], sem.at[k]).wait()
    finish(tiles - 1, (depth - 1) % 2)


BLOCK = 256
GROUP = 4


def place_entries(lab, send, acc, rows_tile, cols_tile, col_devices):
    edges = lab.shape[1]
    wide = GROUP * BLOCK
    upper = (
        lax.broadcasted_iota(I32, (BLOCK, BLOCK), 0) <= lax.broadcasted_iota(I32, (BLOCK, BLOCK), 1)
    ).astype(F32).astype(BF)
    dev = lax.broadcasted_iota(I32, (LANES, BLOCK), 0)
    dev16 = dev.astype(F32).astype(BF)
    one = jnp.ones((LANES, BLOCK), BF)
    zero = jnp.zeros((LANES, BLOCK), BF)
    tail_id = lax.broadcasted_iota(I32, (16, BLOCK), 0) + LANES
    tail16 = tail_id.astype(F32).astype(BF)
    tail_zero = jnp.zeros((16, BLOCK), BF)
    acc[...] = jnp.zeros_like(acc)

    def cast(x):
        return x.astype(F32).astype(BF)

    def group(side):
        def body(u, base):
            lanes = pl.ds(pl.multiple_of(u * wide, wide), wide)
            rlab = lab[pl.ds(side, 1), lanes]
            clab = lab[pl.ds(1 - side, 1), lanes]
            owner = (rlab // rows_tile) * col_devices + clab // cols_tile
            row = rlab % rows_tile + 1
            col = clab % cols_tile
            owner16 = cast(owner)
            pieces = [cast(row >> 5), cast(col >> 5), cast(row & 31), cast(col & 31)]
            hots = []
            for q in range(GROUP):
                cut = slice(q * BLOCK, (q + 1) * BLOCK)
                hots.append(
                    jnp.where(dev16 == jnp.broadcast_to(owner16[:, cut], dev.shape), one, zero)
                )
            within = jnp.dot(jnp.concatenate(hots, 0), upper, preferred_element_type=F32)
            total = jnp.zeros((LANES, 288), F32)
            for q in range(GROUP):
                cut = slice(q * BLOCK, (q + 1) * BLOCK)
                w = within[q * LANES : (q + 1) * LANES]
                running = w + jnp.concatenate([base, base], 1)
                slot = jnp.sum(hots[q].astype(F32) * running, axis=0, keepdims=True) - 1.0
                base = base + jnp.broadcast_to(w[:, BLOCK - 1 :], base.shape)
                slot16 = slot.astype(BF)
                main = dev16 == jnp.broadcast_to(slot16, dev.shape)
                tail = tail16 == jnp.broadcast_to(slot16, tail_id.shape)

                def spread(v):
                    v = v[:, cut]
                    return (
                        jnp.where(main, jnp.broadcast_to(v, dev.shape), zero),
                        jnp.where(tail, jnp.broadcast_to(v, tail_id.shape), tail_zero),
                    )

                rh, ch, rl, cl = [spread(v) for v in pieces]
                high = jnp.concatenate([rh[0], ch[0], rh[1], ch[1]], 0)
                low = jnp.concatenate([rl[0], cl[0], rl[1], cl[1]], 0)
                nt = (((1,), (1,)), ((), ()))
                total += lax.dot_general(hots[q] * 32.0, high, nt, preferred_element_type=F32)
                total += lax.dot_general(hots[q], low, nt, preferred_element_type=F32)
            acc[:, :288] += total
            return base

        return body

    base = jnp.zeros((LANES, LANES), F32)
    for side in (0, 1):
        base = lax.fori_loop(0, edges // wide, group(side), base)
    for k in range(3):
        send[k] = acc[:, k * LANES : (k + 1) * LANES].astype(I32)


def in_blocks(shard, dim, devices):
    before, after = (shard.shape[:dim], shard.shape[dim + 1 :])
    return jnp.moveaxis(shard.reshape(*before, devices, -1, *after), dim, 0)


def summed_on_arrival(shard, axis, dim):
    blocks = in_blocks(shard, dim, lax.axis_size(axis))
    arrived = lax.all_to_all(blocks, axis, split_axis=0, concat_axis=0, tiled=True)
    return arrived.sum(axis=0)


def from_everyone(shard, axis):
    copies = jnp.broadcast_to(shard, (lax.axis_size(axis), *shard.shape))
    return lax.all_to_all(copies, axis, split_axis=0, concat_axis=0, tiled=True)


def over_copies(shard, axis):
    everything = from_everyone(shard, axis)
    return jnp.sum(everything, axis=0)


def packed_total(arrays, axis):
    ends = [0]
    for a in arrays:
        ends.append(ends[-1] + a.size)
    subtotal = over_copies(jnp.concatenate([a.ravel() for a in arrays]), axis)
    return tuple((subtotal[b:e].reshape(a.shape) for a, b, e in zip(arrays, ends, ends[1:])))


def entropy_term(value):
    return value * jnp.log(jnp.maximum(value, 1.0))


def exchange_kernel(row_n, col_n, evm, table, out, lab, hi, s0, s1, s2, s3, g, send, recv, acc, sem, ssem, rsem):
    devices = row_n * col_n
    me = lax.axis_index("row") * col_n + lax.axis_index("col")
    sms = (s0, s1, s2, s3)
    barrier = pltpu.get_barrier_semaphore()

    def greet(k, _):
        d = lax.rem(me + k, devices)
        pl.semaphore_signal(barrier, inc=1, device_id=(d // col_n, lax.rem(d, col_n)), device_id_type=MESH)
        return 0

    lax.fori_loop(1, devices, greet, 0)
    start_gather(evm, hi, sms, sem)
    gather_labels(evm, table, lab, hi, sms, g, sem)
    place_entries(lab, send, acc, BLOCKS // row_n, BLOCKS // col_n, col_n)
    pl.semaphore_wait(barrier, devices - 1)

    def push(k, _):
        d = lax.rem(me + k, devices)
        pltpu.make_async_remote_copy(
            src_ref=send.at[:, pl.ds(d, 1), :],
            dst_ref=recv.at[:, pl.ds(me, 1), :],
            send_sem=ssem,
            recv_sem=rsem,
            device_id=(d // col_n, lax.rem(d, col_n)),
            device_id_type=MESH,
        ).start()
        return 0

    lax.fori_loop(1, devices, push, 0)
    rest = pl.ds(0, devices - 1)
    pltpu.make_async_copy(recv.at[:, rest, :], recv.at[:, rest, :], rsem).wait()
    pltpu.make_async_copy(send.at[:, rest, :], send.at[:, rest, :], ssem).wait()
    own = send[:, pl.ds(me, 1), :]
    recv[:, pl.ds(me, 1), :] = own
    tails = recv[2].T
    out[0, :LANES, :] = recv[0] - 1
    out[1, :LANES, :] = recv[1]
    out[0, LANES:, :] = tails[:16] - 1
    out[1, LANES:, :] = tails[16:32]


def exchange(edge_tiles, labels, row_n, col_n):
    small = pltpu.SMEM((2, LANES), I32)
    return pl.pallas_call(
        functools.partial(exchange_kernel, row_n, col_n),
        out_shape=jax.ShapeDtypeStruct((2, LANES + 16, LANES), I32),
        in_specs=[pl.BlockSpec(memory_space=pltpu.VMEM)] * 2,
        out_specs=pl.BlockSpec(memory_space=pltpu.VMEM),
        scratch_shapes=[
            pltpu.VMEM((2, 4096), I32),
            pltpu.VMEM((32, 2, LANES), I32),
            small,
            small,
            small,
            small,
            pltpu.VMEM((2, 2, LANES, LANES), I32),
            pltpu.VMEM((3, LANES, LANES), I32),
            pltpu.VMEM((3, LANES, LANES), I32),
            pltpu.VMEM((LANES, 384), F32),
            pltpu.SemaphoreType.DMA((4,)),
            pltpu.SemaphoreType.DMA,
            pltpu.SemaphoreType.DMA,
        ],
        compiler_params=pltpu.CompilerParams(collective_id=0, has_side_effects=True),
    )(edge_tiles, labels.reshape(-1, LANES))


def one_hot(v, n):
    wide = v.shape[1]
    ids = lax.broadcasted_iota(I32, (256, wide), 0).astype(F32).astype(BF)
    one = jnp.ones((256, wide), BF)
    zero = jnp.zeros((256, wide), BF)
    out = []
    for b in range(n // 256):
        w = jnp.where((v >> 8) == b, v & 255, -1).astype(F32).astype(BF)
        out.append(jnp.where(ids == jnp.broadcast_to(w, ids.shape), one, zero).astype(F8))
    return jnp.concatenate(out, 0)


STEP = 16


def add_kernel(entries, counts, out):
    out[...] = counts[...]

    def body(i, _):
        r = jnp.concatenate([entries[0, pl.ds(i * STEP + q, 1), :] for q in range(STEP)], 1)
        c = jnp.concatenate([entries[1, pl.ds(i * STEP + q, 1), :] for q in range(STEP)], 1)
        out[...] += lax.dot_general(
            one_hot(r, out.shape[0]),
            one_hot(c, out.shape[1]),
            (((1,), (1,)), ((), ())),
            preferred_element_type=F32,
        )
        return 0

    lax.fori_loop(0, entries.shape[1] // STEP, body, 0)


def add_entries(entries, counts):
    return pl.pallas_call(
        add_kernel,
        out_shape=jax.ShapeDtypeStruct(counts.shape, F32),
        in_specs=[pl.BlockSpec(memory_space=pltpu.VMEM)] * 2,
        out_specs=pl.BlockSpec(memory_space=pltpu.VMEM),
        compiler_params=pltpu.CompilerParams(vmem_limit_bytes=60 << 20),
    )(entries, counts)


def per_device(counts, labels, edge_tiles, proposals, accept_flags):
    rows_tile = counts.shape[0]
    cols_tile = counts.shape[1]
    row_devices = lax.axis_size("row")
    col_devices = lax.axis_size("col")
    row_ids = jnp.arange(rows_tile, dtype=jnp.int32)
    col_ids = jnp.arange(cols_tile, dtype=jnp.int32)
    entries = exchange(edge_tiles, labels, row_devices, col_devices)
    updated = add_entries(entries, counts)
    col_index = lax.axis_index("col")
    row_index = lax.axis_index("row")
    mine = lax.dynamic_slice_in_dim(proposals, col_index * PROP_COL, PROP_COL, 1)
    source = mine[0]
    target = mine[1]
    own_selector = (source[:, None] == col_index * cols_tile + col_ids[None, :]).astype(jnp.float32)
    own_column = lax.dot_general(
        own_selector,
        updated,
        (((1,), (1,)), ((), ())),
        precision=lax.Precision.HIGHEST,
        preferred_element_type=jnp.float32,
    )
    all_targets = proposals[1]
    selector = (all_targets[:, None] == col_index * cols_tile + col_ids[None, :]).astype(
        jnp.float32
    )
    other_column = summed_on_arrival(
        lax.dot_general(
            selector,
            updated,
            (((1,), (1,)), ((), ())),
            precision=lax.Precision.HIGHEST,
            preferred_element_type=jnp.float32,
        ),
        "col",
        0,
    )
    row_global = row_index * rows_tile + row_ids
    at_source = row_global[None, :] == source[:, None]
    at_target = row_global[None, :] == target[:, None]
    mixed = (
        entropy_term(own_column + other_column)
        - entropy_term(own_column)
        - entropy_term(other_column)
    )
    pair_part = jnp.sum(jnp.where(at_source | at_target, jnp.float32(0.0), mixed), axis=1)
    source_part = jnp.sum(jnp.where(at_source, own_column, jnp.float32(0.0)), axis=1)
    cross_part = jnp.sum(jnp.where(at_source, other_column, jnp.float32(0.0)), axis=1)
    target_part = jnp.sum(jnp.where(at_target, other_column, jnp.float32(0.0)), axis=1)
    degree_part = jnp.sum(own_column, axis=1)
    other_degree = jnp.sum(other_column, axis=1)
    pair_sum, self_source, cross_count, self_target, degree_source, degree_target = packed_total(
        (pair_part, source_part, cross_part, target_part, degree_part, other_degree), "row"
    )
    corner = (
        entropy_term(self_source + 2.0 * cross_count + self_target)
        - entropy_term(self_source)
        - entropy_term(self_target)
        - 2.0 * entropy_term(cross_count)
    )
    change = (
        -(pair_sum + 0.5 * corner)
        + entropy_term(degree_source + degree_target)
        - entropy_term(degree_source)
        - entropy_term(degree_target)
    )
    merge_cost = change / BLOCKS
    accepted_cost = jnp.where(accept_flags == 1, merge_cost, jnp.float32(0.0))
    return (updated, merge_cost, accepted_cost)


def solution(mesh):
    return jax.shard_map(
        per_device,
        mesh=mesh,
        in_specs=(P("row", "col"), P(), P(("row", "col"), None, None), P(), P("col")),
        out_specs=(P("row", "col"), P("col"), P("col")),
        check_vma=False,
    )
```

```python
import functools

import jax
import jax.numpy as jnp
from jax import lax
from jax.experimental import pallas as pl
from jax.experimental.pallas import tpu as pltpu
from jax.sharding import PartitionSpec as P

I32 = jnp.int32
F32 = jnp.float32
BF = jnp.bfloat16
F8 = jnp.float8_e4m3fn
LANES = 128
BLOCKS = 8192
MESH = pl.DeviceIdType.MESH


def start_gather(evm, hi, sms, sem):
    hi[...] = lax.shift_right_logical(evm[...], 7)
    for k in range(len(sms)):
        pltpu.make_async_copy(hi.at[k], sms[k], sem.at[k]).start()


def gather_labels(evm, table, lab, hi, sms, g, sem):
    tiles = evm.shape[0]
    depth = len(sms)
    sub = lax.broadcasted_iota(I32, (LANES, LANES), 0)

    def finish(t, slot):
        for side in (0, 1):
            lanes = evm[t, pl.ds(side, 1), :] & (LANES - 1)
            picked = jnp.where(sub == lanes, g[slot, side].T, 0)
            lab[pl.ds(side, 1), pl.ds(pl.multiple_of(t * LANES, LANES), LANES)] = jnp.sum(
                picked, axis=0, keepdims=True
            )

    def body(u, _):
        for k in range(depth):
            t = depth * u + k
            pltpu.make_async_copy(hi.at[t], sms[k], sem.at[k]).wait()
            finish(jnp.maximum(t - 1, 0), (k + 1) % 2)
            for side in (0, 1):
                for e in range(LANES):
                    g[k % 2, side, pl.ds(e, 1), :] = table[pl.ds(sms[k][side, e], 1), :]
            later = jnp.minimum(t + depth, tiles - 1)
            pltpu.make_async_copy(hi.at[later], sms[k], sem.at[k]).start()
        return 0

    lax.fori_loop(0, tiles // depth, body, 0)
    for k in range(depth):
        pltpu.make_async_copy(hi.at[tiles - 1], sms[k], sem.at[k]).wait()
    finish(tiles - 1, (depth - 1) % 2)


BLOCK = 256
GROUP = 4


def place_entries(lab, send, acc, rows_tile, cols_tile, col_devices):
    edges = lab.shape[1]
    wide = GROUP * BLOCK
    upper = (
        lax.broadcasted_iota(I32, (BLOCK, BLOCK), 0) <= lax.broadcasted_iota(I32, (BLOCK, BLOCK), 1)
    ).astype(F32).astype(BF)
    dev = lax.broadcasted_iota(I32, (LANES, BLOCK), 0)
    dev16 = dev.astype(F32).astype(BF)
    one = jnp.ones((LANES, BLOCK), BF)
    zero = jnp.zeros((LANES, BLOCK), BF)
    tail_id = lax.broadcasted_iota(I32, (16, BLOCK), 0) + LANES
    tail16 = tail_id.astype(F32).astype(BF)
    tail_zero = jnp.zeros((16, BLOCK), BF)
    acc[...] = jnp.zeros_like(acc)

    def cast(x):
        return x.astype(F32).astype(BF)

    def group(side):
        def body(u, base):
            lanes = pl.ds(pl.multiple_of(u * wide, wide), wide)
            rlab = lab[pl.ds(side, 1), lanes]
            clab = lab[pl.ds(1 - side, 1), lanes]
            owner = (rlab // rows_tile) * col_devices + clab // cols_tile
            row = rlab % rows_tile + 1
            col = clab % cols_tile
            owner16 = cast(owner)
            pieces = [cast(row >> 5), cast(col >> 5), cast(row & 31), cast(col & 31)]
            hots = []
            for q in range(GROUP):
                cut = slice(q * BLOCK, (q + 1) * BLOCK)
                hots.append(
                    jnp.where(dev16 == jnp.broadcast_to(owner16[:, cut], dev.shape), one, zero)
                )
            within = jnp.dot(jnp.concatenate(hots, 0), upper, preferred_element_type=F32)
            total = jnp.zeros((LANES, 288), F32)
            for q in range(GROUP):
                cut = slice(q * BLOCK, (q + 1) * BLOCK)
                w = within[q * LANES : (q + 1) * LANES]
                running = w + jnp.concatenate([base, base], 1)
                slot = jnp.sum(hots[q].astype(F32) * running, axis=0, keepdims=True) - 1.0
                base = base + jnp.broadcast_to(w[:, BLOCK - 1 :], base.shape)
                slot16 = slot.astype(BF)
                main = dev16 == jnp.broadcast_to(slot16, dev.shape)
                tail = tail16 == jnp.broadcast_to(slot16, tail_id.shape)

                def spread(v):
                    v = v[:, cut]
                    return (
                        jnp.where(main, jnp.broadcast_to(v, dev.shape), zero),
                        jnp.where(tail, jnp.broadcast_to(v, tail_id.shape), tail_zero),
                    )

                rh, ch, rl, cl = [spread(v) for v in pieces]
                high = jnp.concatenate([rh[0], ch[0], rh[1], ch[1]], 0)
                low = jnp.concatenate([rl[0], cl[0], rl[1], cl[1]], 0)
                nt = (((1,), (1,)), ((), ()))
                total += lax.dot_general(hots[q] * 32.0, high, nt, preferred_element_type=F32)
                total += lax.dot_general(hots[q], low, nt, preferred_element_type=F32)
            acc[:, :288] += total
            return base

        return body

    base = jnp.zeros((LANES, LANES), F32)
    for side in (0, 1):
        base = lax.fori_loop(0, edges // wide, group(side), base)
    for k in range(3):
        send[k] = acc[:, k * LANES : (k + 1) * LANES].astype(I32)


def exchange_kernel(row_n, col_n, evm, table, out, lab, hi, s0, s1, s2, s3, g, send, recv, acc, sem, ssem, rsem):
    devices = row_n * col_n
    me = lax.axis_index("row") * col_n + lax.axis_index("col")
    sms = (s0, s1, s2, s3)
    barrier = pltpu.get_barrier_semaphore()

    def greet(k, _):
        d = lax.rem(me + k, devices)
        pl.semaphore_signal(barrier, inc=1, device_id=(d // col_n, lax.rem(d, col_n)), device_id_type=MESH)
        return 0

    lax.fori_loop(1, devices, greet, 0)
    start_gather(evm, hi, sms, sem)
    gather_labels(evm, table, lab, hi, sms, g, sem)
    place_entries(lab, send, acc, BLOCKS // row_n, BLOCKS // col_n, col_n)
    pl.semaphore_wait(barrier, devices - 1)

    def push(k, _):
        d = lax.rem(me + k, devices)
        pltpu.make_async_remote_copy(
            src_ref=send.at[:, pl.ds(d, 1), :],
            dst_ref=recv.at[:, pl.ds(me, 1), :],
            send_sem=ssem,
            recv_sem=rsem,
            device_id=(d // col_n, lax.rem(d, col_n)),
            device_id_type=MESH,
        ).start()
        return 0

    lax.fori_loop(1, devices, push, 0)
    rest = pl.ds(0, devices - 1)
    pltpu.make_async_copy(recv.at[:, rest, :], recv.at[:, rest, :], rsem).wait()
    pltpu.make_async_copy(send.at[:, rest, :], send.at[:, rest, :], ssem).wait()
    own = send[:, pl.ds(me, 1), :]
    recv[:, pl.ds(me, 1), :] = own
    tails = recv[2].T
    out[0, :LANES, :] = recv[0] - 1
    out[1, :LANES, :] = recv[1]
    out[0, LANES:, :] = tails[:16] - 1
    out[1, LANES:, :] = tails[16:32]


def exchange(edge_tiles, labels, row_n, col_n):
    small = pltpu.SMEM((2, LANES), I32)
    return pl.pallas_call(
        functools.partial(exchange_kernel, row_n, col_n),
        out_shape=jax.ShapeDtypeStruct((2, LANES + 16, LANES), I32),
        in_specs=[pl.BlockSpec(memory_space=pltpu.VMEM)] * 2,
        out_specs=pl.BlockSpec(memory_space=pltpu.VMEM),
        scratch_shapes=[
            pltpu.VMEM((2, 4096), I32),
            pltpu.VMEM((32, 2, LANES), I32),
            small,
            small,
            small,
            small,
            pltpu.VMEM((2, 2, LANES, LANES), I32),
            pltpu.VMEM((3, LANES, LANES), I32),
            pltpu.VMEM((3, LANES, LANES), I32),
            pltpu.VMEM((LANES, 384), F32),
            pltpu.SemaphoreType.DMA((4,)),
            pltpu.SemaphoreType.DMA,
            pltpu.SemaphoreType.DMA,
        ],
        compiler_params=pltpu.CompilerParams(collective_id=0, has_side_effects=True),
    )(edge_tiles, labels.reshape(-1, LANES))


def entropy_term(value):
    return value * jnp.log(jnp.maximum(value, 1.0))


def row_code(r, valid, otherwise):
    code = jnp.where(valid, (128 + (r & 127)) << ((r >> 7) & 7), otherwise)
    return code.astype(F32).astype(BF)


def one_hot(v, n):
    wide = v.shape[1]
    ids = lax.broadcasted_iota(I32, (256, wide), 0).astype(F32).astype(BF)
    one = jnp.ones((256, wide), BF)
    zero = jnp.zeros((256, wide), BF)
    out = []
    for b in range(n // 256):
        w = jnp.where((v >> 8) == b, v & 255, -1).astype(F32).astype(BF)
        out.append(jnp.where(ids == jnp.broadcast_to(w, ids.shape), one, zero).astype(F8))
    return jnp.concatenate(out, 0)


STEP = 16
NT = (((1,), (1,)), ((), ()))


def merge_kernel(
    row_n, col_n, early, psm, pvm, flags, entries, counts,
    updated, cost_out, accepted_out,
    columns, picked, col_hot, arrived, packed, finals, ssem, rsem, fssem, frsem,
):
    i = lax.axis_index("row")
    j = lax.axis_index("col")
    rows_tile, cols_tile = counts.shape
    props = psm.shape[1]
    per_row = props // row_n
    steps = entries.shape[1] // STEP
    wide = STEP * LANES
    barrier = pltpu.get_barrier_semaphore()
    home = j // 2

    for k in range(1, row_n):
        pl.semaphore_signal(barrier, inc=1, device_id=(lax.rem(i + k, row_n), j), device_id_type=MESH)

    for k in range(col_n):

        @pl.when(jnp.logical_or(home != i, j != k))
        def _():
            pl.semaphore_signal(barrier, inc=1, device_id=(home, k), device_id_type=MESH)

    for side in (0, 1):
        for h in range(props // LANES):
            line = pvm[side : side + 1, h * LANES : (h + 1) * LANES]
            columns[side, h * LANES : (h + 1) * LANES, :] = jnp.broadcast_to(line, (LANES, LANES)).T
    mine = pl.ds(pl.multiple_of(i * per_row, 8), per_row)
    source = columns[0, mine, :]
    target = columns[1, mine, :]

    def pick(p, _):
        s = psm[1, p] - i * rows_tile
        inside = jnp.logical_and(s >= 0, s < rows_tile)
        line = counts[pl.ds(jnp.clip(s, 0, rows_tile - 1), 1), :]
        picked[pl.ds(p, 1), :] = jnp.where(inside, line, 0.0)
        return 0

    lax.fori_loop(0, props, pick, 0, unroll=8)

    def pick_own(q, _):
        s = psm[0, i * per_row + q] - i * rows_tile
        picked[pl.ds(props + q, 1), :] = counts[pl.ds(jnp.clip(s, 0, rows_tile - 1), 1), :]
        return 0

    lax.fori_loop(0, per_row, pick_own, 0, unroll=8)

    wanted = jnp.concatenate([columns[1], source], 0) - i * rows_tile
    wanted = row_code(wanted, jnp.logical_and(wanted >= 0, wanted < rows_tile), -1)

    def lanes_of(which, s):
        return jnp.concatenate([entries[which, pl.ds(s * STEP + q, 1), :] for q in range(STEP)], 1)

    def small(s, _):
        hot = one_hot(lanes_of(1, s), cols_tile)
        col_hot[s] = hot
        code = row_code(lanes_of(0, s), lanes_of(0, s) >= 0, 0)
        tall = jnp.concatenate([wanted] * STEP, 1)
        match = jnp.where(
            tall == jnp.broadcast_to(code, tall.shape), jnp.ones(tall.shape, BF), jnp.zeros(tall.shape, BF)
        ).astype(F8)
        picked[...] += lax.dot_general(match, hot, NT, preferred_element_type=F32)
        return 0

    lax.fori_loop(0, steps, small, 0)

    @pl.when(home != i)
    def _():
        pl.semaphore_wait(barrier, row_n - 1 + col_n)

    @pl.when(home == i)
    def _():
        pl.semaphore_wait(barrier, row_n - 1 + col_n - 1)

    for k in range(1, row_n):
        d = lax.rem(i + k, row_n)
        pltpu.make_async_remote_copy(
            src_ref=picked.at[pl.ds(pl.multiple_of(d * per_row, 8), per_row), :],
            dst_ref=arrived.at[i],
            send_sem=ssem,
            recv_sem=rsem,
            device_id=(d, j),
            device_id_type=MESH,
        ).start()

    def add(s, _):
        updated[...] += lax.dot_general(
            one_hot(lanes_of(0, s), rows_tile), col_hot[s], NT, preferred_element_type=F32
        )
        return 0

    updated[...] = counts[...]
    lax.fori_loop(0, early, add, 0)

    most = pl.ds(0, row_n - 1)
    pltpu.make_async_copy(arrived.at[most], arrived.at[most], rsem).wait()
    pltpu.make_async_copy(arrived.at[most], arrived.at[most], ssem).wait()
    arrived[i] = picked[mine, :]
    other = jnp.sum(arrived[...], axis=0)
    own = picked[props:, :]
    where_at = lax.broadcasted_iota(I32, own.shape, 1) + j * cols_tile
    wide4 = cols_tile // LANES
    at_source = where_at == jnp.concatenate([source] * wide4, 1)
    at_target = where_at == jnp.concatenate([target] * wide4, 1)
    mixed = entropy_term(own + other) - entropy_term(own) - entropy_term(other)
    parts = (
        jnp.where(jnp.logical_or(at_source, at_target), 0.0, mixed),
        jnp.where(at_source, own, 0.0),
        jnp.where(at_source, other, 0.0),
        jnp.where(at_target, other, 0.0),
        own,
        other,
    )
    lane = lax.broadcasted_iota(I32, (per_row, LANES), 1)
    table = jnp.zeros((per_row, LANES), F32)
    for k, part in enumerate(parts):
        table = jnp.where(lane == k, jnp.sum(part, axis=1, keepdims=True), table)
    table = jnp.concatenate([table, jnp.zeros((LANES - per_row, LANES), F32)], 0).T
    packed[...] = table[:8]

    for k in range(2 * row_n):
        d = (k // 2, 2 * i + k % 2)
        same = jnp.logical_and(d[0] == i, d[1] == j)

        @pl.when(jnp.logical_not(same))
        def _():
            pltpu.make_async_remote_copy(
                src_ref=packed, dst_ref=finals.at[j], send_sem=fssem, recv_sem=frsem,
                device_id=d, device_id_type=MESH,
            ).start()

    @pl.when(home == i)
    def _():
        finals[j] = packed[...]

    lax.fori_loop(early, steps, add, 0)

    @pl.when(home == i)
    def _():
        fewer = pl.ds(0, col_n - 1)
        pltpu.make_async_copy(finals.at[fewer], finals.at[fewer], fssem).wait()
        pltpu.make_async_copy(finals.at[fewer], finals.at[fewer], frsem).wait()

    @pl.when(home != i)
    def _():
        pltpu.make_async_copy(finals, finals, fssem).wait()
        pltpu.make_async_copy(finals, finals, frsem).wait()

    sums = jnp.sum(finals[...], axis=0)
    pair, self_source, cross, self_target, degree_source, degree_target = [
        sums[k : k + 1] for k in range(6)
    ]
    corner = (
        entropy_term(self_source + 2.0 * cross + self_target)
        - entropy_term(self_source)
        - entropy_term(self_target)
        - 2.0 * entropy_term(cross)
    )
    change = (
        -(pair + 0.5 * corner)
        + entropy_term(degree_source + degree_target)
        - entropy_term(degree_source)
        - entropy_term(degree_target)
    )
    cost = change / BLOCKS
    per_col = props // col_n
    cost = jnp.where(lax.rem(j, 2) == 0, cost[:, :per_col], cost[:, per_col : 2 * per_col])
    cost_out[...] = cost
    accepted_out[...] = jnp.where(flags[...] == 1, cost, 0.0)


def merge(proposals, flags, entries, counts, row_n, col_n):
    props = proposals.shape[1]
    per_row = props // row_n
    rows_tile, cols_tile = counts.shape
    vm = pl.BlockSpec(memory_space=pltpu.VMEM)
    out16 = jax.ShapeDtypeStruct(flags.shape, F32)
    return pl.pallas_call(
        functools.partial(merge_kernel, row_n, col_n, 6),
        out_shape=(jax.ShapeDtypeStruct(counts.shape, F32), out16, out16),
        in_specs=[pl.BlockSpec(memory_space=pltpu.SMEM), vm, vm, vm, vm],
        out_specs=(vm, vm, vm),
        scratch_shapes=[
            pltpu.VMEM((2, props, LANES), I32),
            pltpu.VMEM((props + per_row, cols_tile), F32),
            pltpu.VMEM((entries.shape[1] // STEP, cols_tile, STEP * LANES), F8),
            pltpu.VMEM((row_n, per_row, cols_tile), F32),
            pltpu.VMEM((8, LANES), F32),
            pltpu.VMEM((col_n, 8, LANES), F32),
            pltpu.SemaphoreType.DMA,
            pltpu.SemaphoreType.DMA,
            pltpu.SemaphoreType.DMA,
            pltpu.SemaphoreType.DMA,
        ],
        compiler_params=pltpu.CompilerParams(
            collective_id=1, has_side_effects=True, vmem_limit_bytes=60 << 20
        ),
    )(proposals, proposals, flags, entries, counts)


def per_device(counts, labels, edge_tiles, proposals, accept_flags):
    row_n = lax.axis_size("row")
    col_n = lax.axis_size("col")
    entries = exchange(edge_tiles, labels, row_n, col_n)
    updated, cost, accepted = merge(
        proposals, accept_flags.reshape(1, -1), entries, counts, row_n, col_n
    )
    return updated, cost.reshape(-1), accepted.reshape(-1)


def solution(mesh):
    return jax.shard_map(
        per_device,
        mesh=mesh,
        in_specs=(P("row", "col"), P(), P(("row", "col"), None, None), P(), P("col")),
        out_specs=(P("row", "col"), P("col"), P("col")),
        check_vma=False,
    )
```

```python
import functools

import jax
import jax.numpy as jnp
from jax import lax
from jax.experimental import pallas as pl
from jax.experimental.pallas import tpu as pltpu
from jax.sharding import PartitionSpec as P

I32 = jnp.int32
F32 = jnp.float32
BF = jnp.bfloat16
F8 = jnp.float8_e4m3fn
LANES = 128
BLOCKS = 8192
MESH = pl.DeviceIdType.MESH


def start_gather(evm, hi, sms, sem):
    hi[...] = lax.shift_right_logical(evm[...], 7)
    for k in range(len(sms)):
        pltpu.make_async_copy(hi.at[k], sms[k], sem.at[k]).start()


def gather_labels(evm, table, lab, hi, sms, g, sem):
    tiles = evm.shape[0]
    depth = len(sms)
    sub = lax.broadcasted_iota(I32, (LANES, LANES), 0)

    def finish(t, slot):
        for side in (0, 1):
            lanes = evm[t, pl.ds(side, 1), :] & (LANES - 1)
            picked = jnp.where(sub == lanes, g[slot, side].T, 0)
            lab[pl.ds(side, 1), pl.ds(pl.multiple_of(t * LANES, LANES), LANES)] = jnp.sum(
                picked, axis=0, keepdims=True
            )

    def body(u, _):
        for k in range(depth):
            t = depth * u + k
            pltpu.make_async_copy(hi.at[t], sms[k], sem.at[k]).wait()
            finish(jnp.maximum(t - 1, 0), (k + 1) % 2)
            for side in (0, 1):
                for e in range(LANES):
                    g[k % 2, side, pl.ds(e, 1), :] = table[pl.ds(sms[k][side, e], 1), :]
            later = jnp.minimum(t + depth, tiles - 1)
            pltpu.make_async_copy(hi.at[later], sms[k], sem.at[k]).start()
        return 0

    lax.fori_loop(0, tiles // depth, body, 0)
    for k in range(depth):
        pltpu.make_async_copy(hi.at[tiles - 1], sms[k], sem.at[k]).wait()
    finish(tiles - 1, (depth - 1) % 2)


BLOCK = 256
GROUP = 8
NT = (((1,), (1,)), ((), ()))


def place_entries(lab, send, acc, rows_tile, cols_tile, col_devices):
    edges = lab.shape[1]
    wide = GROUP * BLOCK
    upper = (
        lax.broadcasted_iota(I32, (BLOCK, BLOCK), 0) <= lax.broadcasted_iota(I32, (BLOCK, BLOCK), 1)
    ).astype(F32).astype(BF)
    dev16 = lax.broadcasted_iota(I32, (LANES, BLOCK), 0).astype(F32).astype(BF)
    one = jnp.ones((LANES, BLOCK), BF)
    zero = jnp.zeros((LANES, BLOCK), BF)
    tail16 = (lax.broadcasted_iota(I32, (16, BLOCK), 0) + LANES).astype(F32).astype(BF)
    tail_zero = jnp.zeros((16, BLOCK), BF)
    acc[...] = jnp.zeros_like(acc)

    def cast(x):
        return x.astype(F32).astype(BF)

    def group(side):
        def body(u, base):
            lanes = pl.ds(pl.multiple_of(u * wide, wide), wide)
            rlab = lab[pl.ds(side, 1), lanes]
            clab = lab[pl.ds(1 - side, 1), lanes]
            owner16 = cast((rlab // rows_tile) * col_devices + clab // cols_tile)
            row = rlab % rows_tile + 1
            col = clab % cols_tile
            pieces = [cast(row & -32), cast(col & -32), cast(row & 31), cast(col & 31)]
            hots = []
            for q in range(GROUP):
                cut = slice(q * BLOCK, (q + 1) * BLOCK)
                hots.append(
                    jnp.where(dev16 == jnp.broadcast_to(owner16[:, cut], dev16.shape), one, zero)
                )
            within = jnp.dot(jnp.concatenate(hots, 0), upper, preferred_element_type=F32)
            total = None
            for q in range(GROUP):
                cut = slice(q * BLOCK, (q + 1) * BLOCK)
                w = within[q * LANES : (q + 1) * LANES]
                running = w + jnp.concatenate([base, base], 1)
                slot = jnp.sum(hots[q].astype(F32) * running, axis=0, keepdims=True) - 1.0
                base = base + jnp.broadcast_to(w[:, BLOCK - 1 :], base.shape)
                slot16 = slot.astype(BF)
                main = dev16 == jnp.broadcast_to(slot16, dev16.shape)
                tail = tail16 == jnp.broadcast_to(slot16, tail16.shape)
                spread = [
                    jnp.where(main, jnp.broadcast_to(v[:, cut], dev16.shape), zero) for v in pieces
                ] + [
                    jnp.where(tail, jnp.broadcast_to(v[:, cut], tail16.shape), tail_zero) for v in pieces
                ]
                part = lax.dot_general(
                    jnp.concatenate(spread, 0), hots[q], NT, preferred_element_type=F32
                )
                total = part if total is None else total + part
            acc[...] += total
            return base

        return body

    base = jnp.zeros((LANES, LANES), F32)
    for side in (0, 1):
        base = lax.fori_loop(0, edges // wide, group(side), base)
    for k in range(2):
        high = acc[k * LANES : (k + 1) * LANES]
        low = acc[(k + 2) * LANES : (k + 3) * LANES]
        send[k] = (high + low).T.astype(I32)
    tail = acc[4 * LANES : 4 * LANES + 32] + acc[4 * LANES + 32 :]
    send[2] = jnp.concatenate([tail, jnp.zeros((LANES - 32, LANES), F32)], 0).T.astype(I32)


def entropy_term(value):
    return value * jnp.log(jnp.maximum(value, 1.0))


def row_code(r, valid, otherwise):
    code = jnp.where(valid, (128 + (r & 127)) << ((r >> 7) & 7), otherwise)
    return code.astype(F32).astype(BF)


def one_hot(v, n):
    wide = v.shape[1]
    ids = lax.broadcasted_iota(I32, (256, wide), 0).astype(F32).astype(BF)
    one = jnp.ones((256, wide), BF)
    zero = jnp.zeros((256, wide), BF)
    out = []
    for b in range(n // 256):
        w = jnp.where((v >> 8) == b, v & 255, -1).astype(F32).astype(BF)
        out.append(jnp.where(ids == jnp.broadcast_to(w, ids.shape), one, zero).astype(F8))
    return jnp.concatenate(out, 0)


STEP = 16


def ingest_kernel(
    row_n, col_n, early, proposals_in, edges_in, flags_in, table_in, counts_in,
    updated, cost_out, accepted_out,
    table, counts, evm, psm, pvm, flags, lab, hi, s0, s1, s2, s3, g, send, recv, tails, acc,
    columns, picked, col_hot, arrived, packed, finals,
    hsem, lsem, ssem, rsem, essem, ersem, fssem, frsem,
):
    devices = row_n * col_n
    i = lax.axis_index("row")
    j = lax.axis_index("col")
    me = i * col_n + j
    rows_tile, cols_tile = counts.shape
    props = psm.shape[1]
    per_row = props // row_n
    home = j // 2
    sms = (s0, s1, s2, s3)
    barrier = pltpu.get_barrier_semaphore()

    load_table = pltpu.make_async_copy(table_in, table, lsem.at[0])
    load_counts = pltpu.make_async_copy(counts_in, counts, lsem.at[1])
    load_edges = pltpu.make_async_copy(edges_in, evm, lsem.at[2])
    others = (
        pltpu.make_async_copy(proposals_in, pvm, lsem.at[3]),
        pltpu.make_async_copy(proposals_in, psm, lsem.at[4]),
        pltpu.make_async_copy(flags_in, flags, lsem.at[5]),
    )
    load_edges.start()
    load_table.start()
    for load in others:
        load.start()
    load_counts.start()

    def greet(k, _):
        d = lax.rem(me + k, devices)
        pl.semaphore_signal(barrier, inc=1, device_id=(d // col_n, lax.rem(d, col_n)), device_id_type=MESH)
        return 0

    lax.fori_loop(1, devices, greet, 0)
    load_edges.wait()
    start_gather(evm, hi, sms, hsem)
    for load in others:
        load.wait()
    for side in (0, 1):
        for h in range(props // LANES):
            line = pvm[side : side + 1, h * LANES : (h + 1) * LANES]
            columns[side, h * LANES : (h + 1) * LANES, :] = jnp.broadcast_to(line, (LANES, LANES)).T
    load_table.wait()
    gather_labels(evm, table, lab, hi, sms, g, hsem)
    place_entries(lab, send, acc, rows_tile, cols_tile, col_n)
    pl.semaphore_wait(barrier, devices - 1)

    def push(k, _):
        d = lax.rem(me + k, devices)
        pltpu.make_async_remote_copy(
            src_ref=send.at[:, pl.ds(d, 1), :],
            dst_ref=recv.at[:, pl.ds(me, 1), :],
            send_sem=ssem,
            recv_sem=rsem.at[i],
            device_id=(d // col_n, lax.rem(d, col_n)),
            device_id_type=MESH,
        ).start()
        return 0

    lax.fori_loop(1, devices, push, 0)
    recv[:, pl.ds(me, 1), :] = send[:, pl.ds(me, 1), :]
    load_counts.wait()

    def pick(p, _):
        s = psm[1, p] - i * rows_tile
        inside = jnp.logical_and(s >= 0, s < rows_tile)
        line = counts[pl.ds(jnp.clip(s, 0, rows_tile - 1), 1), :]
        picked[pl.ds(p, 1), :] = jnp.where(inside, line, 0.0)
        return 0

    lax.fori_loop(0, props, pick, 0, unroll=8)

    def pick_own(q, _):
        s = psm[0, i * per_row + q] - i * rows_tile
        picked[pl.ds(props + q, 1), :] = counts[pl.ds(jnp.clip(s, 0, rows_tile - 1), 1), :]
        return 0

    lax.fori_loop(0, per_row, pick_own, 0, unroll=8)
    updated[...] = counts[...]

    mine = pl.ds(pl.multiple_of(i * per_row, 8), per_row)
    source = columns[0, mine, :]
    target = columns[1, mine, :]
    wanted = jnp.concatenate([columns[1], source], 0) - i * rows_tile
    wanted = row_code(wanted, jnp.logical_and(wanted >= 0, wanted < rows_tile), -1)

    def lanes_of(ref, s):
        return jnp.concatenate([ref[pl.ds(s * STEP + q, 1), :] for q in range(STEP)], 1)

    def small(s, rows, cols):
        hot = one_hot(cols, cols_tile)
        col_hot[s] = hot
        code = row_code(rows, rows >= 0, 0)
        tall = jnp.concatenate([wanted] * STEP, 1)
        match = jnp.where(
            tall == jnp.broadcast_to(code, tall.shape), jnp.ones(tall.shape, BF), jnp.zeros(tall.shape, BF)
        ).astype(F8)
        picked[...] += lax.dot_general(match, hot, NT, preferred_element_type=F32)

    part = recv.at[:, pl.ds(0, col_n - 1), :]
    pltpu.make_async_copy(part, part, rsem.at[i]).wait()
    small(i, lanes_of(recv.at[0], i) - 1, lanes_of(recv.at[1], i))

    def arrive(k, _):
        s = lax.rem(i - k + row_n, row_n)
        part = recv.at[:, pl.ds(0, col_n), :]
        pltpu.make_async_copy(part, part, rsem.at[s]).wait()
        small(s, lanes_of(recv.at[0], s) - 1, lanes_of(recv.at[1], s))
        return 0

    lax.fori_loop(1, row_n, arrive, 0)
    tails[...] = recv[2].T
    last_rows = jnp.concatenate([tails[q : q + 1] for q in range(16)], 1) - 1
    last_cols = jnp.concatenate([tails[q : q + 1] for q in range(16, 32)], 1)
    small(row_n, last_rows, last_cols)

    for k in range(1, row_n):
        d = lax.rem(i + k, row_n)
        pltpu.make_async_remote_copy(
            src_ref=picked.at[pl.ds(pl.multiple_of(d * per_row, 8), per_row), :],
            dst_ref=arrived.at[i],
            send_sem=essem,
            recv_sem=ersem,
            device_id=(d, j),
            device_id_type=MESH,
        ).start()

    def add(s, rows):
        updated[...] += lax.dot_general(
            one_hot(rows, rows_tile), col_hot[s], NT, preferred_element_type=F32
        )

    def add_step(s, _):
        add(s, lanes_of(recv.at[0], s) - 1)
        return 0

    lax.fori_loop(0, early, add_step, 0)
    rest = pl.ds(0, devices - 1)
    pltpu.make_async_copy(send.at[:, rest, :], send.at[:, rest, :], ssem).wait()

    most = pl.ds(0, row_n - 1)
    pltpu.make_async_copy(arrived.at[most], arrived.at[most], ersem).wait()
    pltpu.make_async_copy(arrived.at[most], arrived.at[most], essem).wait()
    arrived[i] = picked[mine, :]
    other = jnp.sum(arrived[...], axis=0)
    own = picked[props:, :]
    where_at = lax.broadcasted_iota(I32, own.shape, 1) + j * cols_tile
    wide4 = cols_tile // LANES
    at_source = where_at == jnp.concatenate([source] * wide4, 1)
    at_target = where_at == jnp.concatenate([target] * wide4, 1)
    mixed = entropy_term(own + other) - entropy_term(own) - entropy_term(other)
    parts = (
        jnp.where(jnp.logical_or(at_source, at_target), 0.0, mixed),
        jnp.where(at_source, own, 0.0),
        jnp.where(at_source, other, 0.0),
        jnp.where(at_target, other, 0.0),
        own,
        other,
    )
    lane = lax.broadcasted_iota(I32, (per_row, LANES), 1)
    table = jnp.zeros((per_row, LANES), F32)
    for k, part in enumerate(parts):
        table = jnp.where(lane == k, jnp.sum(part, axis=1, keepdims=True), table)
    table = jnp.concatenate([table, jnp.zeros((LANES - per_row, LANES), F32)], 0).T
    packed[...] = table[:8]

    for k in range(2 * row_n):
        d = (k // 2, 2 * i + k % 2)
        same = jnp.logical_and(d[0] == i, d[1] == j)

        @pl.when(jnp.logical_not(same))
        def _():
            pltpu.make_async_remote_copy(
                src_ref=packed, dst_ref=finals.at[j], send_sem=fssem, recv_sem=frsem,
                device_id=d, device_id_type=MESH,
            ).start()

    @pl.when(home == i)
    def _():
        finals[j] = packed[...]

    lax.fori_loop(early, row_n, add_step, 0)
    add(row_n, jnp.concatenate([tails[q : q + 1] for q in range(16)], 1) - 1)

    @pl.when(home == i)
    def _():
        fewer = pl.ds(0, col_n - 1)
        pltpu.make_async_copy(finals.at[fewer], finals.at[fewer], fssem).wait()
        pltpu.make_async_copy(finals.at[fewer], finals.at[fewer], frsem).wait()

    @pl.when(home != i)
    def _():
        pltpu.make_async_copy(finals, finals, fssem).wait()
        pltpu.make_async_copy(finals, finals, frsem).wait()

    sums = jnp.sum(finals[...], axis=0)
    pair, self_source, cross, self_target, degree_source, degree_target = [
        sums[k : k + 1] for k in range(6)
    ]
    corner = (
        entropy_term(self_source + 2.0 * cross + self_target)
        - entropy_term(self_source)
        - entropy_term(self_target)
        - 2.0 * entropy_term(cross)
    )
    change = (
        -(pair + 0.5 * corner)
        + entropy_term(degree_source + degree_target)
        - entropy_term(degree_source)
        - entropy_term(degree_target)
    )
    cost = change / BLOCKS
    per_col = props // col_n
    cost = jnp.where(lax.rem(j, 2) == 0, cost[:, :per_col], cost[:, per_col : 2 * per_col])
    cost_out[...] = cost
    accepted_out[...] = jnp.where(flags[...] == 1, cost, 0.0)


def ingest(proposals, edge_tiles, flags, labels, counts, row_n, col_n):
    props = proposals.shape[1]
    per_row = props // row_n
    rows_tile, cols_tile = counts.shape
    tiles = edge_tiles.shape[0]
    devices = row_n * col_n
    table = labels.reshape(-1, LANES)
    vm = pl.BlockSpec(memory_space=pltpu.VMEM)
    anywhere = pl.BlockSpec(memory_space=pltpu.HBM)
    small = pltpu.SMEM((2, LANES), I32)
    dma = pltpu.SemaphoreType.DMA
    out16 = pltpu.VMEM(flags.shape, F32)
    return pl.pallas_call(
        functools.partial(ingest_kernel, row_n, col_n, 6),
        out_shape=(pltpu.VMEM(counts.shape, F32), out16, out16),
        in_specs=[anywhere] * 5,
        out_specs=(vm, vm, vm),
        scratch_shapes=[
            pltpu.VMEM(table.shape, I32),
            pltpu.VMEM(counts.shape, F32),
            pltpu.VMEM(edge_tiles.shape, I32),
            pltpu.SMEM(proposals.shape, I32),
            pltpu.VMEM(proposals.shape, I32),
            pltpu.VMEM(flags.shape, I32),
            pltpu.VMEM((2, tiles * LANES), I32),
            pltpu.VMEM(edge_tiles.shape, I32),
            small,
            small,
            small,
            small,
            pltpu.VMEM((2, 2, LANES, LANES), I32),
            pltpu.VMEM((3, devices, LANES), I32),
            pltpu.VMEM((3, devices, LANES), I32),
            pltpu.VMEM((LANES, LANES), I32),
            pltpu.VMEM((576, LANES), F32),
            pltpu.VMEM((2, props, LANES), I32),
            pltpu.VMEM((props + per_row, cols_tile), F32),
            pltpu.VMEM((row_n + 1, cols_tile, STEP * LANES), F8),
            pltpu.VMEM((row_n, per_row, cols_tile), F32),
            pltpu.VMEM((8, LANES), F32),
            pltpu.VMEM((col_n, 8, LANES), F32),
            dma((4,)),
            dma((6,)),
            dma,
            dma((row_n,)),
            dma,
            dma,
            dma,
            dma,
        ],
        compiler_params=pltpu.CompilerParams(
            collective_id=0, has_side_effects=True, vmem_limit_bytes=32 << 20
        ),
    )(*[
        pltpu.with_memory_space_constraint(x, pltpu.HBM)
        for x in (proposals, edge_tiles, flags, table, counts)
    ])


def per_device(counts, labels, edge_tiles, proposals, accept_flags):
    row_n = lax.axis_size("row")
    col_n = lax.axis_size("col")
    updated, cost, accepted = ingest(
        proposals, edge_tiles, accept_flags.reshape(1, -1), labels, counts, row_n, col_n
    )
    return updated, cost.reshape(-1), accepted.reshape(-1)


def solution(mesh):
    return jax.shard_map(
        per_device,
        mesh=mesh,
        in_specs=(P("row", "col"), P(), P(("row", "col"), None, None), P(), P("col")),
        out_specs=(P("row", "col"), P("col"), P("col")),
        check_vma=False,
    )
```

```python
import functools

import jax
import jax.numpy as jnp
from jax import lax
from jax.experimental import pallas as pl
from jax.experimental.pallas import tpu as pltpu
from jax.sharding import PartitionSpec as P

I32 = jnp.int32
F32 = jnp.float32
BF = jnp.bfloat16
F8 = jnp.float8_e4m3fn
LANES = 128
BLOCKS = 8192
MESH = pl.DeviceIdType.MESH


def start_gather(evm, hi, sms, sem):
    hi[...] = lax.shift_right_logical(evm[...], 7)
    for k in range(len(sms)):
        pltpu.make_async_copy(hi.at[k], sms[k], sem.at[k]).start()


def gather_labels(evm, table, lab, hi, sms, g, sem):
    tiles = evm.shape[0]
    depth = len(sms)
    sub = lax.broadcasted_iota(I32, (LANES, LANES), 0)

    def finish(t, slot):
        for side in (0, 1):
            lanes = evm[t, pl.ds(side, 1), :] & (LANES - 1)
            picked = jnp.where(sub == lanes, g[slot, side].T, 0)
            lab[side, pl.ds(t, 1), :] = jnp.sum(picked, axis=0, keepdims=True)

    def body(u, _):
        for k in range(depth):
            t = depth * u + k
            pltpu.make_async_copy(hi.at[t], sms[k], sem.at[k]).wait()
            finish(jnp.maximum(t - 1, 0), (k + 1) % 2)
            for side in (0, 1):
                for e in range(LANES):
                    g[k % 2, side, pl.ds(e, 1), :] = table[pl.ds(sms[k][side, e], 1), :]
            later = jnp.minimum(t + depth, tiles - 1)
            pltpu.make_async_copy(hi.at[later], sms[k], sem.at[k]).start()
        return 0

    lax.fori_loop(0, tiles // depth, body, 0)
    for k in range(depth):
        pltpu.make_async_copy(hi.at[tiles - 1], sms[k], sem.at[k]).wait()
    finish(tiles - 1, (depth - 1) % 2)


BLOCK = 256
GROUP = 16
SPREAD = 16
NT = (((1,), (1,)), ((), ()))


def place_entries(lab, enc, hot, slots, send, acc, rows_tile, cols_tile, col_devices):
    tiles = lab.shape[1]
    pair = BLOCK // LANES
    row_bits = rows_tile.bit_length() - 1
    col_bits = cols_tile.bit_length() - 1
    for side in (0, 1):
        row, col = lab[side], lab[1 - side]
        enc[side, 0] = ((row >> row_bits) * col_devices + (col >> col_bits)).astype(F32)
        row = (row & (rows_tile - 1)) + 1
        col = col & (cols_tile - 1)
        for k, piece in enumerate((row & -32, col & -32, row & 31, col & 31)):
            enc[side, k + 1] = piece.astype(F32)
    upper = (
        lax.broadcasted_iota(I32, (BLOCK, BLOCK), 0) <= lax.broadcasted_iota(I32, (BLOCK, BLOCK), 1)
    ).astype(F32).astype(BF)
    dev16 = lax.broadcasted_iota(I32, (LANES, BLOCK), 0).astype(F32).astype(BF)
    one = jnp.ones((LANES, BLOCK), BF)
    zero = jnp.zeros((LANES, BLOCK), BF)
    tail16 = (lax.broadcasted_iota(I32, (16, BLOCK), 0) + LANES).astype(F32).astype(BF)
    tail_zero = jnp.zeros((16, BLOCK), BF)
    acc[...] = jnp.zeros_like(acc)

    def line(ref, q):
        return jnp.concatenate([ref[pl.ds(q * pair + n, 1), :] for n in range(pair)], 1).astype(BF)

    def rank(side):
        def body(u, base):
            hots = []
            for q in range(GROUP):
                owner = line(enc.at[side, 0], u * GROUP + q)
                hots.append(jnp.where(dev16 == jnp.broadcast_to(owner, dev16.shape), one, zero))
            lanes = pl.ds(pl.multiple_of(u * GROUP * BLOCK, GROUP * BLOCK), GROUP * BLOCK)
            hot[side, :, lanes] = jnp.concatenate(hots, 1)
            within = jnp.dot(jnp.concatenate(hots, 0), upper, preferred_element_type=F32)
            for q in range(GROUP):
                w = within[q * LANES : (q + 1) * LANES]
                running = w + jnp.concatenate([base, base], 1)
                slot = jnp.sum(jnp.where(hots[q].astype(F32) > 0.0, running, 0.0), axis=0, keepdims=True) - 1.0
                for n in range(pair):
                    slots[side, pl.ds((u * GROUP + q) * pair + n, 1), :] = slot[:, n * LANES : (n + 1) * LANES]
                base = base + jnp.broadcast_to(w[:, BLOCK - 1 :], base.shape)
            return base

        return body

    def spread(side):
        def body(u, _):
            columns = []
            for q in range(SPREAD):
                at = u * SPREAD + q
                slot = line(slots.at[side], at)
                main = dev16 == jnp.broadcast_to(slot, dev16.shape)
                tail = tail16 == jnp.broadcast_to(slot, tail16.shape)
                pieces = [line(enc.at[side, k], at) for k in range(1, 5)]
                columns.append(
                    jnp.concatenate(
                        [jnp.where(main, jnp.broadcast_to(v, dev16.shape), zero) for v in pieces]
                        + [jnp.where(tail, jnp.broadcast_to(v, tail16.shape), tail_zero) for v in pieces],
                        0,
                    )
                )
            lanes = pl.ds(pl.multiple_of(u * SPREAD * BLOCK, SPREAD * BLOCK), SPREAD * BLOCK)
            acc[...] += lax.dot_general(
                jnp.concatenate(columns, 1), hot[side, :, lanes], NT, preferred_element_type=F32
            )
            return 0

        return body

    base = jnp.zeros((LANES, LANES), F32)
    for side in (0, 1):
        base = lax.fori_loop(0, tiles // (GROUP * pair), rank(side), base)
    for side in (0, 1):
        lax.fori_loop(0, tiles // (SPREAD * pair), spread(side), 0)
    for k in range(2):
        high = acc[k * LANES : (k + 1) * LANES]
        low = acc[(k + 2) * LANES : (k + 3) * LANES]
        send[k] = (high + low).T.astype(I32)
    tail = acc[4 * LANES : 4 * LANES + 32] + acc[4 * LANES + 32 :]
    send[2] = jnp.concatenate([tail, jnp.zeros((LANES - 32, LANES), F32)], 0).T.astype(I32)


def entropy_term(value):
    return value * jnp.log(jnp.maximum(value, 1.0))


def row_code(r, valid, otherwise):
    code = jnp.where(valid, (128 + (r & 127)) << ((r >> 7) & 7), otherwise)
    return code.astype(F32).astype(BF)


def one_hot(v, n):
    wide = v.shape[1]
    ids = lax.broadcasted_iota(I32, (256, wide), 0).astype(F32).astype(BF)
    one = jnp.ones((256, wide), BF)
    zero = jnp.zeros((256, wide), BF)
    out = []
    for b in range(n // 256):
        w = jnp.where((v >> 8) == b, v & 255, -1).astype(F32).astype(BF)
        out.append(jnp.where(ids == jnp.broadcast_to(w, ids.shape), one, zero).astype(F8))
    return jnp.concatenate(out, 0)


STEP = 16


def ingest_kernel(
    row_n, col_n, early, proposals_in, edges_in, flags_in, table_in, counts_in,
    updated, cost_out, accepted_out,
    table, counts, evm, psm, pvm, near, flags, lab, enc, hot, slots, hi, s0, s1, s2, s3, g, send, recv, tails, acc,
    columns, picked, col_hot, arrived, packed, finals,
    hsem, lsem, ssem, rsem, essem, ersem, fssem, frsem,
):
    devices = row_n * col_n
    i = lax.axis_index("row")
    j = lax.axis_index("col")
    me = i * col_n + j
    rows_tile, cols_tile = counts.shape
    props = pvm.shape[1]
    per_row = props // row_n
    home = j // 2
    sms = (s0, s1, s2, s3)
    barrier = pltpu.get_barrier_semaphore()

    load_table = pltpu.make_async_copy(table_in, table, lsem.at[0])
    load_counts = pltpu.make_async_copy(counts_in, counts, lsem.at[1])
    load_edges = pltpu.make_async_copy(edges_in, evm, lsem.at[2])
    others = (
        pltpu.make_async_copy(proposals_in, pvm, lsem.at[3]),
        pltpu.make_async_copy(flags_in, flags, lsem.at[5]),
    )
    load_edges.start()
    load_updated = pltpu.make_async_copy(counts_in, updated, lsem.at[6])
    load_near = pltpu.make_async_copy(near, psm, lsem.at[4])
    load_table.start()
    for load in others:
        load.start()

    def peer(r, c):
        return lax.rem(i + r, row_n), lax.rem(j + c, col_n)

    def greet(r, _, first=0):
        for c in range(first, col_n):
            pl.semaphore_signal(barrier, inc=1, device_id=peer(r, c), device_id_type=MESH)
        return 0

    greet(0, 0, 1)
    lax.fori_loop(1, row_n, greet, 0)
    load_edges.wait()
    start_gather(evm, hi, sms, hsem)
    for load in others:
        load.wait()
    near[...] = jnp.clip(pvm[...] - i * rows_tile, 0, rows_tile - 1)
    load_near.start()
    for side in (0, 1):
        for h in range(props // LANES):
            line = pvm[side : side + 1, h * LANES : (h + 1) * LANES]
            columns[side, h * LANES : (h + 1) * LANES, :] = jnp.broadcast_to(line, (LANES, LANES)).T
    load_near.wait()
    load_table.wait()
    load_counts.start()
    load_updated.start()
    gather_labels(evm, table, lab, hi, sms, g, hsem)
    place_entries(lab, enc, hot, slots, send, acc, rows_tile, cols_tile, col_n)
    pl.semaphore_wait(barrier, devices - 1)

    def push(r, _, first=0):
        for c in range(first, col_n):
            d = peer(r, c)
            at = pl.ds(d[0] * col_n + d[1], 1)
            pltpu.make_async_remote_copy(
                src_ref=send.at[:, at, :],
                dst_ref=recv.at[:, pl.ds(me, 1), :],
                send_sem=ssem,
                recv_sem=rsem.at[i],
                device_id=d,
                device_id_type=MESH,
            ).start()
        return 0

    push(0, 0, 1)
    lax.fori_loop(1, row_n, push, 0)
    recv[:, pl.ds(me, 1), :] = send[:, pl.ds(me, 1), :]
    load_counts.wait()

    def pick(u, _):
        for q in range(8):
            p = u * 8 + q
            picked[pl.ds(p, 1), :] = counts[pl.ds(psm[1, p], 1), :]
        return 0

    lax.fori_loop(0, props // 8, pick, 0)
    for q in range(per_row):
        picked[props + q : props + q + 1, :] = counts[pl.ds(psm[0, i * per_row + q], 1), :]
    apart = columns[1] - i * rows_tile
    inside = jnp.logical_and(apart >= 0, apart < rows_tile)
    picked[:props, :] = jnp.where(
        jnp.concatenate([inside] * (cols_tile // LANES), 1), picked[:props, :], 0.0
    )

    mine = pl.ds(pl.multiple_of(i * per_row, 8), per_row)
    source = columns[0, mine, :]
    target = columns[1, mine, :]
    wanted = jnp.concatenate([columns[1], source], 0) - i * rows_tile
    wanted = row_code(wanted, jnp.logical_and(wanted >= 0, wanted < rows_tile), -1)

    def lanes_of(ref, s):
        return jnp.concatenate([ref[pl.ds(s * STEP + q, 1), :] for q in range(STEP)], 1)

    def small(s, rows, cols):
        hot = one_hot(cols, cols_tile)
        col_hot[s] = hot
        code = row_code(rows, rows >= 0, 0)
        tall = jnp.concatenate([wanted] * STEP, 1)
        match = jnp.where(
            tall == jnp.broadcast_to(code, tall.shape), jnp.ones(tall.shape, BF), jnp.zeros(tall.shape, BF)
        ).astype(F8)
        picked[...] += lax.dot_general(match, hot, NT, preferred_element_type=F32)

    part = recv.at[:, pl.ds(0, col_n - 1), :]
    pltpu.make_async_copy(part, part, rsem.at[i]).wait()
    small(i, lanes_of(recv.at[0], i) - 1, lanes_of(recv.at[1], i))

    def arrive(k, _):
        s = lax.rem(i - k + row_n, row_n)
        part = recv.at[:, pl.ds(0, col_n), :]
        pltpu.make_async_copy(part, part, rsem.at[s]).wait()
        small(s, lanes_of(recv.at[0], s) - 1, lanes_of(recv.at[1], s))
        return 0

    lax.fori_loop(1, row_n, arrive, 0)
    tails[...] = recv[2].T
    last_rows = jnp.concatenate([tails[q : q + 1] for q in range(16)], 1) - 1
    last_cols = jnp.concatenate([tails[q : q + 1] for q in range(16, 32)], 1)
    small(row_n, last_rows, last_cols)

    for k in range(1, row_n):
        d = lax.rem(i + k, row_n)
        pltpu.make_async_remote_copy(
            src_ref=picked.at[pl.ds(pl.multiple_of(d * per_row, 8), per_row), :],
            dst_ref=arrived.at[i],
            send_sem=essem,
            recv_sem=ersem,
            device_id=(d, j),
            device_id_type=MESH,
        ).start()

    def add(s, rows):
        updated[...] += lax.dot_general(
            one_hot(rows, rows_tile), col_hot[s], NT, preferred_element_type=F32
        )

    def add_step(s, _):
        add(s, lanes_of(recv.at[0], s) - 1)
        return 0

    load_updated.wait()
    lax.fori_loop(0, early, add_step, 0)
    rest = pl.ds(0, devices - 1)
    pltpu.make_async_copy(send.at[:, rest, :], send.at[:, rest, :], ssem).wait()

    most = pl.ds(0, row_n - 1)
    pltpu.make_async_copy(arrived.at[most], arrived.at[most], ersem).wait()
    pltpu.make_async_copy(arrived.at[most], arrived.at[most], essem).wait()
    arrived[i] = picked[mine, :]
    other = jnp.sum(arrived[...], axis=0)
    own = picked[props:, :]
    where_at = lax.broadcasted_iota(I32, own.shape, 1) + j * cols_tile
    wide4 = cols_tile // LANES
    at_source = where_at == jnp.concatenate([source] * wide4, 1)
    at_target = where_at == jnp.concatenate([target] * wide4, 1)
    mixed = entropy_term(own + other) - entropy_term(own) - entropy_term(other)
    parts = (
        jnp.where(jnp.logical_or(at_source, at_target), 0.0, mixed),
        jnp.where(at_source, own, 0.0),
        jnp.where(at_source, other, 0.0),
        jnp.where(at_target, other, 0.0),
        own,
        other,
    )
    lane = lax.broadcasted_iota(I32, (per_row, LANES), 1)
    table = jnp.zeros((per_row, LANES), F32)
    for k, part in enumerate(parts):
        table = jnp.where(lane == k, jnp.sum(part, axis=1, keepdims=True), table)
    table = jnp.concatenate([table, jnp.zeros((LANES - per_row, LANES), F32)], 0).T
    packed[...] = table[:8]

    for k in range(2 * row_n):
        d = (k // 2, 2 * i + k % 2)
        same = jnp.logical_and(d[0] == i, d[1] == j)

        @pl.when(jnp.logical_not(same))
        def _():
            pltpu.make_async_remote_copy(
                src_ref=packed, dst_ref=finals.at[j], send_sem=fssem, recv_sem=frsem,
                device_id=d, device_id_type=MESH,
            ).start()

    @pl.when(home == i)
    def _():
        finals[j] = packed[...]

    lax.fori_loop(early, row_n, add_step, 0)
    add(row_n, jnp.concatenate([tails[q : q + 1] for q in range(16)], 1) - 1)

    @pl.when(home == i)
    def _():
        fewer = pl.ds(0, col_n - 1)
        pltpu.make_async_copy(finals.at[fewer], finals.at[fewer], fssem).wait()
        pltpu.make_async_copy(finals.at[fewer], finals.at[fewer], frsem).wait()

    @pl.when(home != i)
    def _():
        pltpu.make_async_copy(finals, finals, fssem).wait()
        pltpu.make_async_copy(finals, finals, frsem).wait()

    sums = jnp.sum(finals[...], axis=0)
    pair, self_source, cross, self_target, degree_source, degree_target = [
        sums[k : k + 1] for k in range(6)
    ]
    corner = (
        entropy_term(self_source + 2.0 * cross + self_target)
        - entropy_term(self_source)
        - entropy_term(self_target)
        - 2.0 * entropy_term(cross)
    )
    change = (
        -(pair + 0.5 * corner)
        + entropy_term(degree_source + degree_target)
        - entropy_term(degree_source)
        - entropy_term(degree_target)
    )
    cost = change / BLOCKS
    per_col = props // col_n
    cost = jnp.where(lax.rem(j, 2) == 0, cost[:, :per_col], cost[:, per_col : 2 * per_col])
    cost_out[...] = cost
    accepted_out[...] = jnp.where(flags[...] == 1, cost, 0.0)


def ingest(proposals, edge_tiles, flags, labels, counts, row_n, col_n):
    props = proposals.shape[1]
    per_row = props // row_n
    rows_tile, cols_tile = counts.shape
    tiles = edge_tiles.shape[0]
    devices = row_n * col_n
    table = labels.reshape(-1, LANES)
    vm = pl.BlockSpec(memory_space=pltpu.VMEM)
    anywhere = pl.BlockSpec(memory_space=pltpu.HBM)
    small = pltpu.SMEM((2, LANES), I32)
    dma = pltpu.SemaphoreType.DMA
    out16 = pltpu.VMEM(flags.shape, F32)
    return pl.pallas_call(
        functools.partial(ingest_kernel, row_n, col_n, 6),
        out_shape=(pltpu.VMEM(counts.shape, F32), out16, out16),
        in_specs=[anywhere] * 5,
        out_specs=(vm, vm, vm),
        scratch_shapes=[
            pltpu.VMEM(table.shape, I32),
            pltpu.VMEM(counts.shape, F32),
            pltpu.VMEM(edge_tiles.shape, I32),
            pltpu.SMEM(proposals.shape, I32),
            pltpu.VMEM(proposals.shape, I32),
            pltpu.VMEM(proposals.shape, I32),
            pltpu.VMEM(flags.shape, I32),
            pltpu.VMEM((2, tiles, LANES), I32),
            pltpu.VMEM((2, 5, tiles, LANES), F32),
            pltpu.VMEM((2, LANES, tiles * LANES), BF),
            pltpu.VMEM((2, tiles, LANES), F32),
            pltpu.VMEM(edge_tiles.shape, I32),
            small,
            small,
            small,
            small,
            pltpu.VMEM((2, 2, LANES, LANES), I32),
            pltpu.VMEM((3, devices, LANES), I32),
            pltpu.VMEM((3, devices, LANES), I32),
            pltpu.VMEM((LANES, LANES), I32),
            pltpu.VMEM((576, LANES), F32),
            pltpu.VMEM((2, props, LANES), I32),
            pltpu.VMEM((props + per_row, cols_tile), F32),
            pltpu.VMEM((row_n + 1, cols_tile, STEP * LANES), F8),
            pltpu.VMEM((row_n, per_row, cols_tile), F32),
            pltpu.VMEM((8, LANES), F32),
            pltpu.VMEM((col_n, 8, LANES), F32),
            dma((4,)),
            dma((7,)),
            dma,
            dma((row_n,)),
            dma,
            dma,
            dma,
            dma,
        ],
        compiler_params=pltpu.CompilerParams(
            collective_id=0, has_side_effects=True, vmem_limit_bytes=32 << 20
        ),
    )(*[
        pltpu.with_memory_space_constraint(x, pltpu.HBM)
        for x in (proposals, edge_tiles, flags, table, counts)
    ])


def finish_kernel(updated_in, cost_in, accepted_in, updated, cost, accepted, sem):
    copy = pltpu.make_async_copy(updated_in, updated, sem)
    copy.start()
    cost[...] = cost_in[...]
    accepted[...] = accepted_in[...]
    copy.wait()


def per_device(counts, labels, edge_tiles, proposals, accept_flags):
    row_n = lax.axis_size("row")
    col_n = lax.axis_size("col")
    flags = accept_flags.reshape(1, -1)
    parts = ingest(proposals, edge_tiles, flags, labels, counts, row_n, col_n)
    vm = pl.BlockSpec(memory_space=pltpu.VMEM)
    out16 = jax.ShapeDtypeStruct(flags.shape, F32)
    updated, cost, accepted = pl.pallas_call(
        finish_kernel,
        out_shape=(jax.ShapeDtypeStruct(counts.shape, F32), out16, out16),
        in_specs=[vm] * 3,
        out_specs=(pl.BlockSpec(memory_space=pltpu.HBM), vm, vm),
        scratch_shapes=[pltpu.SemaphoreType.DMA],
        compiler_params=pltpu.CompilerParams(vmem_limit_bytes=8 << 20),
    )(*parts)
    return updated, cost.reshape(-1), accepted.reshape(-1)


def solution(mesh):
    return jax.shard_map(
        per_device,
        mesh=mesh,
        in_specs=(P("row", "col"), P(), P(("row", "col"), None, None), P(), P("col")),
        out_specs=(P("row", "col"), P("col"), P("col")),
        check_vma=False,
    )
```

```python
import functools

import jax
import jax.numpy as jnp
from jax import lax
from jax.experimental import pallas as pl
from jax.experimental.pallas import tpu as pltpu
from jax.sharding import PartitionSpec as P

I32 = jnp.int32
F32 = jnp.float32
BF = jnp.bfloat16
F8 = jnp.float8_e4m3fn
LANES = 128
BLOCKS = 8192
MESH = pl.DeviceIdType.MESH


def start_gather(evm, hi, sms, sem):
    hi[...] = lax.shift_right_logical(evm[...], 7)
    for k in range(len(sms)):
        pltpu.make_async_copy(hi.at[k], sms[k], sem.at[k]).start()


def gather_labels(evm, table, lab, hi, sms, g, sem):
    tiles = evm.shape[0]
    depth = len(sms)
    sub = lax.broadcasted_iota(I32, (LANES, LANES), 0)

    def finish(t, slot):
        for side in (0, 1):
            lanes = evm[t, pl.ds(side, 1), :] & (LANES - 1)
            picked = jnp.where(sub == lanes, g[slot, side].T, 0)
            lab[side, pl.ds(t, 1), :] = jnp.sum(picked, axis=0, keepdims=True)

    def body(u, _):
        for k in range(depth):
            t = depth * u + k
            pltpu.make_async_copy(hi.at[t], sms[k], sem.at[k]).wait()
            finish(jnp.maximum(t - 1, 0), (k + 1) % 2)
            for side in (0, 1):
                for e in range(LANES):
                    g[k % 2, side, pl.ds(e, 1), :] = table[pl.ds(sms[k][side, e], 1), :]
            later = jnp.minimum(t + depth, tiles - 1)
            pltpu.make_async_copy(hi.at[later], sms[k], sem.at[k]).start()
        return 0

    lax.fori_loop(0, tiles // depth, body, 0)
    for k in range(depth):
        pltpu.make_async_copy(hi.at[tiles - 1], sms[k], sem.at[k]).wait()
    finish(tiles - 1, (depth - 1) % 2)


BLOCK = 256
GROUP = 16
SPREAD = 16
NT = (((1,), (1,)), ((), ()))


def place_entries(lab, enc, hot, slots, send, acc, rows_tile, cols_tile, col_devices):
    tiles = lab.shape[1]
    pair = BLOCK // LANES
    row_bits = rows_tile.bit_length() - 1
    col_bits = cols_tile.bit_length() - 1
    for side in (0, 1):
        row, col = lab[side], lab[1 - side]
        enc[side, 0] = ((row >> row_bits) * col_devices + (col >> col_bits)).astype(F32)
        row = (row & (rows_tile - 1)) + 1
        col = col & (cols_tile - 1)
        for k, piece in enumerate((row & -32, col & -32, row & 31, col & 31)):
            enc[side, k + 1] = piece.astype(F32)
    upper = (
        lax.broadcasted_iota(I32, (BLOCK, BLOCK), 0) <= lax.broadcasted_iota(I32, (BLOCK, BLOCK), 1)
    ).astype(F32).astype(BF)
    dev16 = lax.broadcasted_iota(I32, (LANES, BLOCK), 0).astype(F32).astype(BF)
    one = jnp.ones((LANES, BLOCK), BF)
    zero = jnp.zeros((LANES, BLOCK), BF)
    tail16 = (lax.broadcasted_iota(I32, (16, BLOCK), 0) + LANES).astype(F32).astype(BF)
    tail_zero = jnp.zeros((16, BLOCK), BF)
    acc[...] = jnp.zeros_like(acc)

    def line(ref, q):
        return jnp.concatenate([ref[pl.ds(q * pair + n, 1), :] for n in range(pair)], 1).astype(BF)

    def rank(side):
        def body(u, base):
            hots = []
            for q in range(GROUP):
                owner = line(enc.at[side, 0], u * GROUP + q)
                hots.append(jnp.where(dev16 == jnp.broadcast_to(owner, dev16.shape), one, zero))
            lanes = pl.ds(pl.multiple_of(u * GROUP * BLOCK, GROUP * BLOCK), GROUP * BLOCK)
            hot[side, :, lanes] = jnp.concatenate(hots, 1)
            within = jnp.dot(jnp.concatenate(hots, 0), upper, preferred_element_type=F32)
            for q in range(GROUP):
                w = within[q * LANES : (q + 1) * LANES]
                running = w + jnp.concatenate([base, base], 1)
                slot = jnp.sum(jnp.where(hots[q].astype(F32) > 0.0, running, 0.0), axis=0, keepdims=True) - 1.0
                for n in range(pair):
                    slots[side, pl.ds((u * GROUP + q) * pair + n, 1), :] = slot[:, n * LANES : (n + 1) * LANES]
                base = base + jnp.broadcast_to(w[:, BLOCK - 1 :], base.shape)
            return base

        return body

    def spread(side):
        def body(u, _):
            columns = []
            for q in range(SPREAD):
                at = u * SPREAD + q
                slot = line(slots.at[side], at)
                main = dev16 == jnp.broadcast_to(slot, dev16.shape)
                tail = tail16 == jnp.broadcast_to(slot, tail16.shape)
                pieces = [line(enc.at[side, k], at) for k in range(1, 5)]
                columns.append(
                    jnp.concatenate(
                        [jnp.where(main, jnp.broadcast_to(v, dev16.shape), zero) for v in pieces]
                        + [jnp.where(tail, jnp.broadcast_to(v, tail16.shape), tail_zero) for v in pieces],
                        0,
                    )
                )
            lanes = pl.ds(pl.multiple_of(u * SPREAD * BLOCK, SPREAD * BLOCK), SPREAD * BLOCK)
            acc[...] += lax.dot_general(
                jnp.concatenate(columns, 1), hot[side, :, lanes], NT, preferred_element_type=F32
            )
            return 0

        return body

    base = jnp.zeros((LANES, LANES), F32)
    for side in (0, 1):
        base = lax.fori_loop(0, tiles // (GROUP * pair), rank(side), base)
    for side in (0, 1):
        lax.fori_loop(0, tiles // (SPREAD * pair), spread(side), 0)
    for k in range(2):
        high = acc[k * LANES : (k + 1) * LANES]
        low = acc[(k + 2) * LANES : (k + 3) * LANES]
        send[k] = (high + low).T.astype(I32)
    tail = acc[4 * LANES : 4 * LANES + 32] + acc[4 * LANES + 32 :]
    send[2] = jnp.concatenate([tail, jnp.zeros((LANES - 32, LANES), F32)], 0).T.astype(I32)


def entropy_term(value):
    return value * jnp.log(jnp.maximum(value, 1.0))


def row_code(r, valid, otherwise):
    code = jnp.where(valid, (128 + (r & 127)) << ((r >> 7) & 7), otherwise)
    return code.astype(F32).astype(BF)


def one_hot(v, n):
    wide = v.shape[1]
    ids = lax.broadcasted_iota(I32, (256, wide), 0).astype(F32).astype(BF)
    one = jnp.ones((256, wide), BF)
    zero = jnp.zeros((256, wide), BF)
    out = []
    for b in range(n // 256):
        w = jnp.where((v >> 8) == b, v & 255, -1).astype(F32).astype(BF)
        out.append(jnp.where(ids == jnp.broadcast_to(w, ids.shape), one, zero).astype(F8))
    return jnp.concatenate(out, 0)


STEP = 16
TABLE_PARTS = 6


def ingest_kernel(
    row_n, col_n, early, proposals_in, edges_in, flags_in, table_in, counts_in,
    updated, cost_out, accepted_out,
    table, counts, evm, psm, pvm, near, flags, lab, enc, hot, slots, hi, s0, s1, s2, s3, g, send, recv, tails, acc,
    columns, picked, col_hot, halves, merged, arrived, packed, finals,
    hsem, lsem, tsem, ssem, rsem, essem, ersem, fssem, frsem,
):
    devices = row_n * col_n
    i = lax.axis_index("row")
    j = lax.axis_index("col")
    me = i * col_n + j
    place_of = lax.rem(j, 4) * (col_n // 4) + j // 4
    my_slot = place_of * row_n + i
    my_group = my_slot // STEP
    rows_tile, cols_tile = counts.shape
    props = pvm.shape[1]
    per_row = props // row_n
    home = j // 2
    sms = (s0, s1, s2, s3)
    barrier = pltpu.get_barrier_semaphore()

    pieces = [pl.ds(k * (table.shape[0] // TABLE_PARTS), table.shape[0] // TABLE_PARTS) for k in range(TABLE_PARTS)]
    load_table = [pltpu.make_async_copy(table_in.at[p], table.at[p], tsem.at[k]) for k, p in enumerate(pieces)]
    load_counts = pltpu.make_async_copy(counts_in, counts, lsem.at[1])
    load_edges = pltpu.make_async_copy(edges_in, evm, lsem.at[2])
    others = (
        pltpu.make_async_copy(proposals_in, pvm, lsem.at[3]),
        pltpu.make_async_copy(flags_in, flags, lsem.at[5]),
    )
    load_edges.start()
    load_updated = pltpu.make_async_copy(counts_in, updated, lsem.at[6])
    load_near = pltpu.make_async_copy(near, psm, lsem.at[4])
    for load in load_table:
        load.start()
    for load in others:
        load.start()

    def peer(r, c):
        return lax.rem(i + r, row_n), lax.rem(j + c, col_n)

    def greet(r, _, first=0):
        for c in range(first, col_n):
            pl.semaphore_signal(barrier, inc=1, device_id=peer(r, c), device_id_type=MESH)
        return 0

    greet(0, 0, 1)
    lax.fori_loop(1, row_n, greet, 0)
    load_edges.wait()
    start_gather(evm, hi, sms, hsem)
    for load in others:
        load.wait()
    near[...] = jnp.clip(pvm[...] - i * rows_tile, 0, rows_tile - 1)
    load_near.start()
    for side in (0, 1):
        for h in range(props // LANES):
            line = pvm[side : side + 1, h * LANES : (h + 1) * LANES]
            columns[side, h * LANES : (h + 1) * LANES, :] = jnp.broadcast_to(line, (LANES, LANES)).T
    load_near.wait()
    for load in load_table:
        load.wait()
    load_counts.start()
    load_updated.start()
    gather_labels(evm, table, lab, hi, sms, g, hsem)
    place_entries(lab, enc, hot, slots, send, acc, rows_tile, cols_tile, col_n)
    pl.semaphore_wait(barrier, devices - 1)

    def push(r, _, first=0):
        for c in range(first, col_n):
            d = peer(r, c)
            at = pl.ds(d[0] * col_n + d[1], 1)
            pltpu.make_async_remote_copy(
                src_ref=send.at[:, at, :],
                dst_ref=recv.at[:, pl.ds(my_slot, 1), :],
                send_sem=ssem,
                recv_sem=rsem.at[my_group],
                device_id=d,
                device_id_type=MESH,
            ).start()
        return 0

    push(0, 0, 1)
    lax.fori_loop(1, row_n, push, 0)
    recv[:, pl.ds(my_slot, 1), :] = send[:, pl.ds(me, 1), :]
    load_counts.wait()

    def pick(u, _):
        for q in range(8):
            p = u * 8 + q
            picked[pl.ds(p, 1), :] = counts[pl.ds(psm[1, p], 1), :]
        return 0

    lax.fori_loop(0, props // 8, pick, 0)
    for q in range(per_row):
        picked[props + q : props + q + 1, :] = counts[pl.ds(psm[0, i * per_row + q], 1), :]
    apart = columns[1] - i * rows_tile
    inside = jnp.logical_and(apart >= 0, apart < rows_tile)
    picked[:props, :] = jnp.where(
        jnp.concatenate([inside] * (cols_tile // LANES), 1), picked[:props, :], 0.0
    )

    mine = pl.ds(pl.multiple_of(i * per_row, 8), per_row)
    source = columns[0, mine, :]
    target = columns[1, mine, :]
    wanted = jnp.concatenate([columns[1], source], 0) - i * rows_tile
    wanted = row_code(wanted, jnp.logical_and(wanted >= 0, wanted < rows_tile), -1)

    def lanes_of(ref, s):
        return jnp.concatenate([ref[pl.ds(s * STEP + q, 1), :] for q in range(STEP)], 1)

    def small(s, rows, cols):
        hot = one_hot(cols, cols_tile)
        col_hot[s] = hot
        code = row_code(rows, rows >= 0, 0)
        tall = jnp.concatenate([wanted] * STEP, 1)
        match = jnp.where(
            tall == jnp.broadcast_to(code, tall.shape), jnp.ones(tall.shape, BF), jnp.zeros(tall.shape, BF)
        ).astype(F8)
        picked[...] += lax.dot_general(match, hot, NT, preferred_element_type=F32)

    groups = devices // STEP

    def arrive(s, _):
        @pl.when(s == my_group)
        def _():
            part = recv.at[:, pl.ds(0, STEP - 1), :]
            pltpu.make_async_copy(part, part, rsem.at[s]).wait()

        @pl.when(s != my_group)
        def _():
            part = recv.at[:, pl.ds(0, STEP), :]
            pltpu.make_async_copy(part, part, rsem.at[s]).wait()

        small(s, lanes_of(recv.at[0], s) - 1, lanes_of(recv.at[1], s))
        return 0

    lax.fori_loop(0, groups, arrive, 0)
    tails[...] = recv[2].T
    last_rows = jnp.concatenate([tails[q : q + 1] for q in range(16)], 1) - 1
    last_cols = jnp.concatenate([tails[q : q + 1] for q in range(16, 32)], 1)
    small(groups, last_rows, last_cols)

    x = i // 2
    core = lax.rem(i, 2)
    chips = row_n // 2

    def chunk(k, c):
        return pl.ds(pl.multiple_of((lax.rem(x + k, chips) * 2 + c) * per_row, 8), per_row)

    def first(k):
        return pltpu.make_async_remote_copy(
            src_ref=picked.at[chunk(k, 1 - core), :],
            dst_ref=halves.at[k],
            send_sem=essem.at[k],
            recv_sem=ersem.at[k],
            device_id=(x * 2 + 1 - core, j),
            device_id_type=MESH,
        )

    def second(k):
        return pltpu.make_async_remote_copy(
            src_ref=merged.at[k],
            dst_ref=arrived.at[k],
            send_sem=essem.at[chips + k],
            recv_sem=ersem.at[chips + k],
            device_id=(lax.rem(x + k, chips) * 2 + core, j),
            device_id_type=MESH,
        )

    far_first = (2, 1, 3, 0)
    for k in far_first:
        first(k).start()

    def add(s, rows):
        updated[...] += lax.dot_general(
            one_hot(rows, rows_tile), col_hot[s], NT, preferred_element_type=F32
        )

    def add_step(s, _):
        add(s, lanes_of(recv.at[0], s) - 1)
        return 0

    load_updated.wait()
    lax.fori_loop(0, 1, add_step, 0)
    for k in far_first:
        first(k).wait_recv()
        merged[k] = picked[chunk(k, core), :] + halves[k]
        if k > 0:
            second(k).start()
    lax.fori_loop(1, early, add_step, 0)
    rest = pl.ds(0, devices - 1)
    pltpu.make_async_copy(send.at[:, rest, :], send.at[:, rest, :], ssem).wait()

    other = merged[0]
    for k in range(chips):
        first(k).wait_send()
        if k > 0:
            second(k).wait()
            other += arrived[k]
    own = picked[props:, :]
    where_at = lax.broadcasted_iota(I32, own.shape, 1) + j * cols_tile
    wide4 = cols_tile // LANES
    at_source = where_at == jnp.concatenate([source] * wide4, 1)
    at_target = where_at == jnp.concatenate([target] * wide4, 1)
    mixed = entropy_term(own + other) - entropy_term(own) - entropy_term(other)
    parts = (
        jnp.where(jnp.logical_or(at_source, at_target), 0.0, mixed),
        jnp.where(at_source, own, 0.0),
        jnp.where(at_source, other, 0.0),
        jnp.where(at_target, other, 0.0),
        own,
        other,
    )
    lane = lax.broadcasted_iota(I32, (per_row, LANES), 1)
    table = jnp.zeros((per_row, LANES), F32)
    for k, part in enumerate(parts):
        table = jnp.where(lane == k, jnp.sum(part, axis=1, keepdims=True), table)
    table = jnp.concatenate([table, jnp.zeros((LANES - per_row, LANES), F32)], 0).T
    packed[...] = table[:8]

    for k in range(2 * row_n):
        d = (k // 2, 2 * i + k % 2)
        same = jnp.logical_and(d[0] == i, d[1] == j)

        @pl.when(jnp.logical_not(same))
        def _():
            pltpu.make_async_remote_copy(
                src_ref=packed, dst_ref=finals.at[j], send_sem=fssem, recv_sem=frsem,
                device_id=d, device_id_type=MESH,
            ).start()

    @pl.when(home == i)
    def _():
        finals[j] = packed[...]

    lax.fori_loop(early, groups, add_step, 0)
    add(groups, jnp.concatenate([tails[q : q + 1] for q in range(16)], 1) - 1)

    @pl.when(home == i)
    def _():
        fewer = pl.ds(0, col_n - 1)
        pltpu.make_async_copy(finals.at[fewer], finals.at[fewer], fssem).wait()
        pltpu.make_async_copy(finals.at[fewer], finals.at[fewer], frsem).wait()

    @pl.when(home != i)
    def _():
        pltpu.make_async_copy(finals, finals, fssem).wait()
        pltpu.make_async_copy(finals, finals, frsem).wait()

    sums = jnp.sum(finals[...], axis=0)
    pair, self_source, cross, self_target, degree_source, degree_target = [
        sums[k : k + 1] for k in range(6)
    ]
    corner = (
        entropy_term(self_source + 2.0 * cross + self_target)
        - entropy_term(self_source)
        - entropy_term(self_target)
        - 2.0 * entropy_term(cross)
    )
    change = (
        -(pair + 0.5 * corner)
        + entropy_term(degree_source + degree_target)
        - entropy_term(degree_source)
        - entropy_term(degree_target)
    )
    cost = change / BLOCKS
    per_col = props // col_n
    cost = jnp.where(lax.rem(j, 2) == 0, cost[:, :per_col], cost[:, per_col : 2 * per_col])
    cost_out[...] = cost
    accepted_out[...] = jnp.where(flags[...] == 1, cost, 0.0)


def ingest(proposals, edge_tiles, flags, labels, counts, row_n, col_n):
    props = proposals.shape[1]
    per_row = props // row_n
    rows_tile, cols_tile = counts.shape
    tiles = edge_tiles.shape[0]
    devices = row_n * col_n
    table = labels.reshape(-1, LANES)
    vm = pl.BlockSpec(memory_space=pltpu.VMEM)
    anywhere = pl.BlockSpec(memory_space=pltpu.HBM)
    small = pltpu.SMEM((2, LANES), I32)
    dma = pltpu.SemaphoreType.DMA
    out16 = pltpu.VMEM(flags.shape, F32)
    return pl.pallas_call(
        functools.partial(ingest_kernel, row_n, col_n, 5),
        out_shape=(pltpu.VMEM(counts.shape, F32), out16, out16),
        in_specs=[anywhere] * 5,
        out_specs=(vm, vm, vm),
        scratch_shapes=[
            pltpu.VMEM(table.shape, I32),
            pltpu.VMEM(counts.shape, F32),
            pltpu.VMEM(edge_tiles.shape, I32),
            pltpu.SMEM(proposals.shape, I32),
            pltpu.VMEM(proposals.shape, I32),
            pltpu.VMEM(proposals.shape, I32),
            pltpu.VMEM(flags.shape, I32),
            pltpu.VMEM((2, tiles, LANES), I32),
            pltpu.VMEM((2, 5, tiles, LANES), F32),
            pltpu.VMEM((2, LANES, tiles * LANES), BF),
            pltpu.VMEM((2, tiles, LANES), F32),
            pltpu.VMEM(edge_tiles.shape, I32),
            small,
            small,
            small,
            small,
            pltpu.VMEM((2, 2, LANES, LANES), I32),
            pltpu.VMEM((3, devices, LANES), I32),
            pltpu.VMEM((3, devices, LANES), I32),
            pltpu.VMEM((LANES, LANES), I32),
            pltpu.VMEM((576, LANES), F32),
            pltpu.VMEM((2, props, LANES), I32),
            pltpu.VMEM((props + per_row, cols_tile), F32),
            pltpu.VMEM((devices // STEP + 1, cols_tile, STEP * LANES), F8),
            pltpu.VMEM((row_n // 2, per_row, cols_tile), F32),
            pltpu.VMEM((row_n // 2, per_row, cols_tile), F32),
            pltpu.VMEM((row_n // 2, per_row, cols_tile), F32),
            pltpu.VMEM((8, LANES), F32),
            pltpu.VMEM((col_n, 8, LANES), F32),
            dma((4,)),
            dma((7,)),
            dma((TABLE_PARTS,)),
            dma,
            dma((devices // STEP,)),
            dma((row_n,)),
            dma((row_n,)),
            dma,
            dma,
        ],
        compiler_params=pltpu.CompilerParams(
            collective_id=0, has_side_effects=True, vmem_limit_bytes=32 << 20
        ),
    )(*[
        pltpu.with_memory_space_constraint(x, pltpu.HBM)
        for x in (proposals, edge_tiles, flags, table, counts)
    ])


def finish_kernel(updated_in, cost_in, accepted_in, updated, cost, accepted, sem):
    copy = pltpu.make_async_copy(updated_in, updated, sem)
    copy.start()
    cost[...] = cost_in[...]
    accepted[...] = accepted_in[...]
    copy.wait()


def per_device(counts, labels, edge_tiles, proposals, accept_flags):
    row_n = lax.axis_size("row")
    col_n = lax.axis_size("col")
    flags = accept_flags.reshape(1, -1)
    parts = ingest(proposals, edge_tiles, flags, labels, counts, row_n, col_n)
    vm = pl.BlockSpec(memory_space=pltpu.VMEM)
    out16 = jax.ShapeDtypeStruct(flags.shape, F32)
    updated, cost, accepted = pl.pallas_call(
        finish_kernel,
        out_shape=(jax.ShapeDtypeStruct(counts.shape, F32), out16, out16),
        in_specs=[vm] * 3,
        out_specs=(pl.BlockSpec(memory_space=pltpu.HBM), vm, vm),
        scratch_shapes=[pltpu.SemaphoreType.DMA],
        compiler_params=pltpu.CompilerParams(vmem_limit_bytes=8 << 20),
    )(*parts)
    return updated, cost.reshape(-1), accepted.reshape(-1)


def solution(mesh):
    return jax.shard_map(
        per_device,
        mesh=mesh,
        in_specs=(P("row", "col"), P(), P(("row", "col"), None, None), P(), P("col")),
        out_specs=(P("row", "col"), P("col"), P("col")),
        check_vma=False,
    )
```

```python
import functools

import jax
import jax.numpy as jnp
from jax import lax
from jax.experimental import pallas as pl
from jax.experimental.pallas import tpu as pltpu
from jax.sharding import PartitionSpec as P

I32 = jnp.int32
F32 = jnp.float32
BF = jnp.bfloat16
F8 = jnp.float8_e4m3fn
LANES = 128
BLOCKS = 8192
MESH = pl.DeviceIdType.MESH


def start_gather(evm, hi, sms, sem):
    hi[...] = lax.shift_right_logical(evm[...], 7)
    for k in range(len(sms)):
        pltpu.make_async_copy(hi.at[k], sms[k], sem.at[k]).start()


def gather_labels(evm, table, lab, hi, sms, g, sem):
    tiles = evm.shape[0]
    depth = len(sms)
    sub = lax.broadcasted_iota(I32, (LANES, LANES), 0)

    def finish(t, slot):
        for side in (0, 1):
            lanes = evm[t, pl.ds(side, 1), :] & (LANES - 1)
            picked = jnp.where(sub == lanes, g[slot, side].T, 0)
            lab[side, pl.ds(t, 1), :] = jnp.sum(picked, axis=0, keepdims=True)

    def body(u, _):
        for k in range(depth):
            t = depth * u + k
            pltpu.make_async_copy(hi.at[t], sms[k], sem.at[k]).wait()
            finish(jnp.maximum(t - 1, 0), (k + 1) % 2)
            for side in (0, 1):
                for e in range(LANES):
                    g[k % 2, side, pl.ds(e, 1), :] = table[pl.ds(sms[k][side, e], 1), :]
            later = jnp.minimum(t + depth, tiles - 1)
            pltpu.make_async_copy(hi.at[later], sms[k], sem.at[k]).start()
        return 0

    lax.fori_loop(0, tiles // depth, body, 0)
    for k in range(depth):
        pltpu.make_async_copy(hi.at[tiles - 1], sms[k], sem.at[k]).wait()
    finish(tiles - 1, (depth - 1) % 2)


BLOCK = 256
GROUP = 16
SPREAD = 16
NT = (((1,), (1,)), ((), ()))


def place_entries(lab, enc, hot, slots, send, acc, rows_tile, cols_tile, col_devices):
    tiles = lab.shape[1]
    pair = BLOCK // LANES
    row_bits = rows_tile.bit_length() - 1
    col_bits = cols_tile.bit_length() - 1
    for side in (0, 1):
        row, col = lab[side], lab[1 - side]
        enc[side, 0] = ((row >> row_bits) * col_devices + (col >> col_bits)).astype(F32)
        row = (row & (rows_tile - 1)) + 1
        col = col & (cols_tile - 1)
        for k, piece in enumerate((row & -32, col & -32, row & 31, col & 31)):
            enc[side, k + 1] = piece.astype(F32)
    upper = (
        lax.broadcasted_iota(I32, (BLOCK, BLOCK), 0) <= lax.broadcasted_iota(I32, (BLOCK, BLOCK), 1)
    ).astype(F32).astype(BF)
    dev32 = lax.broadcasted_iota(I32, (LANES, BLOCK), 0).astype(F32)
    dev16 = dev32.astype(BF)
    one = jnp.ones((LANES, BLOCK), BF)
    zero = jnp.zeros((LANES, BLOCK), BF)
    tail16 = (lax.broadcasted_iota(I32, (16, BLOCK), 0) + LANES).astype(F32).astype(BF)
    tail_zero = jnp.zeros((16, BLOCK), BF)
    acc[...] = jnp.zeros_like(acc)

    def line(ref, q, kind=BF):
        return jnp.concatenate([ref[pl.ds(q * pair + n, 1), :] for n in range(pair)], 1).astype(kind)

    def rank(side):
        def body(u, base):
            hots = []
            for q in range(GROUP):
                owner = line(enc.at[side, 0], u * GROUP + q)
                hots.append(jnp.where(dev16 == jnp.broadcast_to(owner, dev16.shape), one, zero))
            lanes = pl.ds(pl.multiple_of(u * GROUP * BLOCK, GROUP * BLOCK), GROUP * BLOCK)
            hot[side, :, lanes] = jnp.concatenate(hots, 1)
            within = jnp.dot(jnp.concatenate(hots, 0), upper, preferred_element_type=F32)
            for q in range(GROUP):
                w = within[q * LANES : (q + 1) * LANES]
                running = w + jnp.concatenate([base, base], 1)
                owner = line(enc.at[side, 0], u * GROUP + q, F32)
                here = dev32 == jnp.broadcast_to(owner, dev32.shape)
                slot = jnp.sum(jnp.where(here, running, 0.0), axis=0, keepdims=True) - 1.0
                for n in range(pair):
                    slots[side, pl.ds((u * GROUP + q) * pair + n, 1), :] = slot[:, n * LANES : (n + 1) * LANES]
                base = base + jnp.broadcast_to(w[:, BLOCK - 1 :], base.shape)
            return base

        return body

    def spread(side):
        def body(u, _):
            columns = []
            for q in range(SPREAD):
                at = u * SPREAD + q
                slot = line(slots.at[side], at)
                main = dev16 == jnp.broadcast_to(slot, dev16.shape)
                tail = tail16 == jnp.broadcast_to(slot, tail16.shape)
                pieces = [line(enc.at[side, k], at) for k in range(1, 5)]
                columns.append(
                    jnp.concatenate(
                        [jnp.where(main, jnp.broadcast_to(v, dev16.shape), zero) for v in pieces]
                        + [jnp.where(tail, jnp.broadcast_to(v, tail16.shape), tail_zero) for v in pieces],
                        0,
                    )
                )
            lanes = pl.ds(pl.multiple_of(u * SPREAD * BLOCK, SPREAD * BLOCK), SPREAD * BLOCK)
            acc[...] += lax.dot_general(
                jnp.concatenate(columns, 1), hot[side, :, lanes], NT, preferred_element_type=F32
            )
            return 0

        return body

    base = jnp.zeros((LANES, LANES), F32)
    for side in (0, 1):
        base = lax.fori_loop(0, tiles // (GROUP * pair), rank(side), base)
    for side in (0, 1):
        lax.fori_loop(0, tiles // (SPREAD * pair), spread(side), 0)
    for k in range(2):
        high = acc[k * LANES : (k + 1) * LANES]
        low = acc[(k + 2) * LANES : (k + 3) * LANES]
        send[k] = (high + low).T.astype(I32)
    tail = acc[4 * LANES : 4 * LANES + 32] + acc[4 * LANES + 32 :]
    send[2] = jnp.concatenate([tail, jnp.zeros((LANES - 32, LANES), F32)], 0).T.astype(I32)


def entropy_term(value):
    return value * jnp.log(jnp.maximum(value, 1.0))


def row_code(r, valid, otherwise):
    code = jnp.where(valid, (128 + (r & 127)) << ((r >> 7) & 7), otherwise)
    return code.astype(F32).astype(BF)


def one_hot(v, n):
    wide = v.shape[1]
    ids = lax.broadcasted_iota(I32, (256, wide), 0).astype(F32).astype(BF)
    one = jnp.ones((256, wide), BF)
    zero = jnp.zeros((256, wide), BF)
    out = []
    for b in range(n // 256):
        w = jnp.where((v >> 8) == b, v & 255, -1).astype(F32).astype(BF)
        out.append(jnp.where(ids == jnp.broadcast_to(w, ids.shape), one.astype(F8), zero.astype(F8)))
    return jnp.concatenate(out, 0)


STEP = 16
TABLE_PARTS = 6
FAR_FIRST = ((2, 2), (1, 2), (2, 1), (2, 3), (3, 2), (0, 2), (1, 1), (1, 3), (2, 0), (3, 1), (3, 3), (0, 1), (0, 3), (1, 0), (3, 0), (0, 0))


def ingest_kernel(
    row_n, col_n, early, proposals_in, edges_in, flags_in, table_in, counts_in,
    updated, cost_out, accepted_out,
    table, counts, evm, psm, pvm, near, flags, lab, enc, hot, slots, hi, s0, s1, s2, s3, g, send, recv, tails, acc,
    columns, picked, col_hot, halves, merged, arrived, packed, finals,
    hsem, lsem, tsem, ssem, rsem, essem, ersem, fssem, frsem,
):
    devices = row_n * col_n
    i = lax.axis_index("row")
    j = lax.axis_index("col")
    me = i * col_n + j
    place_of = lax.rem(j, 4) * (col_n // 4) + j // 4
    my_slot = place_of * row_n + i
    my_group = my_slot // STEP
    rows_tile, cols_tile = counts.shape
    props = pvm.shape[1]
    per_row = props // row_n
    home = j // 2
    sms = (s0, s1, s2, s3)
    barrier = pltpu.get_barrier_semaphore()

    pieces = [pl.ds(k * (table.shape[0] // TABLE_PARTS), table.shape[0] // TABLE_PARTS) for k in range(TABLE_PARTS)]
    load_table = [pltpu.make_async_copy(table_in.at[p], table.at[p], tsem.at[k]) for k, p in enumerate(pieces)]
    load_counts = pltpu.make_async_copy(counts_in, counts, lsem.at[1])
    load_edges = pltpu.make_async_copy(edges_in, evm, lsem.at[2])
    others = (
        pltpu.make_async_copy(proposals_in, pvm, lsem.at[3]),
        pltpu.make_async_copy(flags_in, flags, lsem.at[5]),
    )
    load_edges.start()
    load_updated = pltpu.make_async_copy(counts_in, updated, lsem.at[6])
    load_near = pltpu.make_async_copy(near, psm, lsem.at[4])
    for load in load_table:
        load.start()
    for load in others:
        load.start()

    def peer(r, c):
        return lax.rem(i + r, row_n), lax.rem(j + c, col_n)

    def greet(r, _, first=0):
        for c in range(first, col_n):
            pl.semaphore_signal(barrier, inc=1, device_id=peer(r, c), device_id_type=MESH)
        return 0

    greet(0, 0, 1)
    lax.fori_loop(1, row_n, greet, 0)
    load_edges.wait()
    start_gather(evm, hi, sms, hsem)
    for load in others:
        load.wait()
    near[...] = jnp.clip(pvm[...] - i * rows_tile, 0, rows_tile - 1)
    load_near.start()
    for side in (0, 1):
        for h in range(props // LANES):
            line = pvm[side : side + 1, h * LANES : (h + 1) * LANES]
            columns[side, h * LANES : (h + 1) * LANES, :] = jnp.broadcast_to(line, (LANES, LANES)).T
    load_near.wait()
    for load in load_table:
        load.wait()
    load_counts.start()
    load_updated.start()
    gather_labels(evm, table, lab, hi, sms, g, hsem)
    place_entries(lab, enc, hot, slots, send, acc, rows_tile, cols_tile, col_n)
    pl.semaphore_wait(barrier, devices - 1)

    def push(t, _, last=0):
        r = row_n // 2 + (t + 1) // 2 * (2 * lax.rem(t, 2) - 1)
        row = lax.rem(i + r, row_n)
        for dz, dy in FAR_FIRST[: len(FAR_FIRST) - last]:
            col = lax.rem(j // 4 + dz, 4) * 4 + lax.rem(j + dy, 4)
            pltpu.make_async_remote_copy(
                src_ref=send.at[:, pl.ds(row * col_n + col, 1), :],
                dst_ref=recv.at[:, pl.ds(my_slot, 1), :],
                send_sem=ssem,
                recv_sem=rsem.at[my_group],
                device_id=(row, col),
                device_id_type=MESH,
            ).start()
        return 0

    lax.fori_loop(0, row_n - 1, push, 0)
    push(row_n - 1, 0, 1)
    recv[:, pl.ds(my_slot, 1), :] = send[:, pl.ds(me, 1), :]
    load_counts.wait()

    def pick(u, _):
        block = picked.at[pl.ds(pl.multiple_of(u * 8, 8), 8), :]
        for q in range(8):
            block[q : q + 1, :] = counts[pl.ds(psm[1, u * 8 + q], 1), :]
        return 0

    lax.fori_loop(0, props // 8, pick, 0)
    for q in range(per_row):
        picked[props + q : props + q + 1, :] = counts[pl.ds(psm[0, i * per_row + q], 1), :]
    apart = columns[1] - i * rows_tile
    inside = jnp.logical_and(apart >= 0, apart < rows_tile)
    picked[:props, :] = jnp.where(
        jnp.concatenate([inside] * (cols_tile // LANES), 1), picked[:props, :], 0.0
    )

    mine = pl.ds(pl.multiple_of(i * per_row, 8), per_row)
    source = columns[0, mine, :]
    target = columns[1, mine, :]
    wanted = jnp.concatenate([columns[1], source], 0) - i * rows_tile
    wanted = row_code(wanted, jnp.logical_and(wanted >= 0, wanted < rows_tile), -1)

    def lanes_of(ref, s):
        return jnp.concatenate([ref[pl.ds(s * STEP + q, 1), :] for q in range(STEP)], 1)

    def small(s, rows, cols):
        hot = one_hot(cols, cols_tile)
        col_hot[s] = hot
        code = row_code(rows, rows >= 0, 0)
        tall = jnp.concatenate([wanted] * STEP, 1)
        match = jnp.where(
            tall == jnp.broadcast_to(code, tall.shape), jnp.ones(tall.shape, BF), jnp.zeros(tall.shape, BF)
        ).astype(F8)
        picked[...] += lax.dot_general(match, hot, NT, preferred_element_type=F32)

    groups = devices // STEP

    def arrive(s, _):
        @pl.when(s == my_group)
        def _():
            part = recv.at[:, pl.ds(0, STEP - 1), :]
            pltpu.make_async_copy(part, part, rsem.at[s]).wait()

        @pl.when(s != my_group)
        def _():
            part = recv.at[:, pl.ds(0, STEP), :]
            pltpu.make_async_copy(part, part, rsem.at[s]).wait()

        small(s, lanes_of(recv.at[0], s) - 1, lanes_of(recv.at[1], s))
        return 0

    lax.fori_loop(0, groups, arrive, 0)
    tails[...] = recv[2].T
    last_rows = jnp.concatenate([tails[q : q + 1] for q in range(16)], 1) - 1
    last_cols = jnp.concatenate([tails[q : q + 1] for q in range(16, 32)], 1)
    small(groups, last_rows, last_cols)

    x = i // 2
    core = lax.rem(i, 2)
    chips = row_n // 2

    def chunk(k, c):
        return pl.ds(pl.multiple_of((lax.rem(x + k, chips) * 2 + c) * per_row, 8), per_row)

    def first(k):
        return pltpu.make_async_remote_copy(
            src_ref=picked.at[chunk(k, 1 - core), :],
            dst_ref=halves.at[k],
            send_sem=essem.at[k],
            recv_sem=ersem.at[k],
            device_id=(x * 2 + 1 - core, j),
            device_id_type=MESH,
        )

    def second(k):
        return pltpu.make_async_remote_copy(
            src_ref=merged.at[k],
            dst_ref=arrived.at[k],
            send_sem=essem.at[chips + k],
            recv_sem=ersem.at[chips + k],
            device_id=(lax.rem(x + k, chips) * 2 + core, j),
            device_id_type=MESH,
        )

    far_first = (2, 1, 3, 0)
    for k in far_first:
        first(k).start()

    def add(s, rows):
        updated[...] += lax.dot_general(
            one_hot(rows, rows_tile), col_hot[s], NT, preferred_element_type=F32
        )

    def add_step(s, _):
        add(s, lanes_of(recv.at[0], s) - 1)
        return 0

    load_updated.wait()
    lax.fori_loop(0, 1, add_step, 0)
    for k in far_first:
        first(k).wait_recv()
        merged[k] = picked[chunk(k, core), :] + halves[k]
        if k > 0:
            second(k).start()
    lax.fori_loop(1, early, add_step, 0)
    rest = pl.ds(0, devices - 1)
    pltpu.make_async_copy(send.at[:, rest, :], send.at[:, rest, :], ssem).wait()

    other = merged[0]
    for k in range(chips):
        first(k).wait_send()
        if k > 0:
            second(k).wait()
            other += arrived[k]
    own = picked[props:, :]
    where_at = lax.broadcasted_iota(I32, own.shape, 1) + j * cols_tile
    wide4 = cols_tile // LANES
    at_source = where_at == jnp.concatenate([source] * wide4, 1)
    at_target = where_at == jnp.concatenate([target] * wide4, 1)
    mixed = entropy_term(own + other) - entropy_term(own) - entropy_term(other)
    parts = (
        jnp.where(jnp.logical_or(at_source, at_target), 0.0, mixed),
        jnp.where(at_source, own, 0.0),
        jnp.where(at_source, other, 0.0),
        jnp.where(at_target, other, 0.0),
        own,
        other,
    )
    half = per_row // 2
    lane = lax.broadcasted_iota(I32, (per_row, LANES), 1)
    table6 = jnp.zeros((per_row, LANES), F32)
    for k, part in enumerate(parts):
        table6 = jnp.where((lane >> (half.bit_length() - 1)) == k, jnp.sum(part, axis=1, keepdims=True), table6)
    row = lax.broadcasted_iota(I32, (per_row, LANES), 0)
    table6 = jnp.where((lane & (half - 1)) == (row & (half - 1)), table6, 0.0)
    for h in range(2):
        packed[h] = jnp.sum(table6[h * half : (h + 1) * half], axis=0, keepdims=True)

    for k in range(2 * row_n):
        d = (k // 2, 2 * i + k % 2)
        same = jnp.logical_and(d[0] == i, d[1] == j)

        @pl.when(jnp.logical_not(same))
        def _():
            pltpu.make_async_remote_copy(
                src_ref=packed.at[k % 2], dst_ref=finals.at[j], send_sem=fssem, recv_sem=frsem,
                device_id=d, device_id_type=MESH,
            ).start()

    @pl.when(home == i)
    def _():
        finals[j] = packed[lax.rem(j, 2)]

    lax.fori_loop(early, groups, add_step, 0)
    add(groups, jnp.concatenate([tails[q : q + 1] for q in range(16)], 1) - 1)

    @pl.when(home == i)
    def _():
        fewer = pl.ds(0, col_n - 1)
        pltpu.make_async_copy(finals.at[fewer], finals.at[fewer], fssem).wait()
        pltpu.make_async_copy(finals.at[fewer], finals.at[fewer], frsem).wait()

    @pl.when(home != i)
    def _():
        pltpu.make_async_copy(finals, finals, fssem).wait()
        pltpu.make_async_copy(finals, finals, frsem).wait()

    sums = jnp.sum(finals[...], axis=0)
    per_col = props // col_n
    pair, self_source, cross, self_target, degree_source, degree_target = [
        sums[:, k * per_col : (k + 1) * per_col] for k in range(6)
    ]
    corner = (
        entropy_term(self_source + 2.0 * cross + self_target)
        - entropy_term(self_source)
        - entropy_term(self_target)
        - 2.0 * entropy_term(cross)
    )
    change = (
        -(pair + 0.5 * corner)
        + entropy_term(degree_source + degree_target)
        - entropy_term(degree_source)
        - entropy_term(degree_target)
    )
    cost = change / BLOCKS
    cost_out[...] = cost
    accepted_out[...] = jnp.where(flags[...] == 1, cost, 0.0)


def ingest(proposals, edge_tiles, flags, labels, counts, row_n, col_n):
    props = proposals.shape[1]
    per_row = props // row_n
    rows_tile, cols_tile = counts.shape
    tiles = edge_tiles.shape[0]
    devices = row_n * col_n
    table = labels.reshape(-1, LANES)
    vm = pl.BlockSpec(memory_space=pltpu.VMEM)
    anywhere = pl.BlockSpec(memory_space=pltpu.HBM)
    small = pltpu.SMEM((2, LANES), I32)
    dma = pltpu.SemaphoreType.DMA
    out16 = pltpu.VMEM(flags.shape, F32)
    return pl.pallas_call(
        functools.partial(ingest_kernel, row_n, col_n, 5),
        out_shape=(pltpu.VMEM(counts.shape, F32), out16, out16),
        in_specs=[anywhere] * 5,
        out_specs=(vm, vm, vm),
        scratch_shapes=[
            pltpu.VMEM(table.shape, I32),
            pltpu.VMEM(counts.shape, F32),
            pltpu.VMEM(edge_tiles.shape, I32),
            pltpu.SMEM(proposals.shape, I32),
            pltpu.VMEM(proposals.shape, I32),
            pltpu.VMEM(proposals.shape, I32),
            pltpu.VMEM(flags.shape, I32),
            pltpu.VMEM((2, tiles, LANES), I32),
            pltpu.VMEM((2, 5, tiles, LANES), F32),
            pltpu.VMEM((2, LANES, tiles * LANES), BF),
            pltpu.VMEM((2, tiles, LANES), F32),
            pltpu.VMEM(edge_tiles.shape, I32),
            small,
            small,
            small,
            small,
            pltpu.VMEM((2, 2, LANES, LANES), I32),
            pltpu.VMEM((3, devices, LANES), I32),
            pltpu.VMEM((3, devices, LANES), I32),
            pltpu.VMEM((LANES, LANES), I32),
            pltpu.VMEM((576, LANES), F32),
            pltpu.VMEM((2, props, LANES), I32),
            pltpu.VMEM((props + per_row, cols_tile), F32),
            pltpu.VMEM((devices // STEP + 1, cols_tile, STEP * LANES), F8),
            pltpu.VMEM((row_n // 2, per_row, cols_tile), F32),
            pltpu.VMEM((row_n // 2, per_row, cols_tile), F32),
            pltpu.VMEM((row_n // 2, per_row, cols_tile), F32),
            pltpu.VMEM((2, 1, LANES), F32),
            pltpu.VMEM((col_n, 1, LANES), F32),
            dma((4,)),
            dma((7,)),
            dma((TABLE_PARTS,)),
            dma,
            dma((devices // STEP,)),
            dma((row_n,)),
            dma((row_n,)),
            dma,
            dma,
        ],
        compiler_params=pltpu.CompilerParams(
            collective_id=0,
            has_side_effects=True,
            vmem_limit_bytes=32 << 20,
        ),
    )(*[
        pltpu.with_memory_space_constraint(x, pltpu.HBM)
        for x in (proposals, edge_tiles, flags, table, counts)
    ])


def finish_kernel(updated_in, cost_in, accepted_in, updated, cost, accepted, sem):
    copy = pltpu.make_async_copy(updated_in, updated, sem)
    copy.start()
    cost[...] = cost_in[...]
    accepted[...] = accepted_in[...]
    copy.wait()


def per_device(counts, labels, edge_tiles, proposals, accept_flags):
    row_n = lax.axis_size("row")
    col_n = lax.axis_size("col")
    flags = accept_flags.reshape(1, -1)
    parts = ingest(proposals, edge_tiles, flags, labels, counts, row_n, col_n)
    vm = pl.BlockSpec(memory_space=pltpu.VMEM)
    out16 = jax.ShapeDtypeStruct(flags.shape, F32)
    updated, cost, accepted = pl.pallas_call(
        finish_kernel,
        out_shape=(jax.ShapeDtypeStruct(counts.shape, F32), out16, out16),
        in_specs=[vm] * 3,
        out_specs=(pl.BlockSpec(memory_space=pltpu.HBM), vm, vm),
        scratch_shapes=[pltpu.SemaphoreType.DMA],
        compiler_params=pltpu.CompilerParams(vmem_limit_bytes=8 << 20),
    )(*parts)
    return updated, cost.reshape(-1), accepted.reshape(-1)


def solution(mesh):
    return jax.shard_map(
        per_device,
        mesh=mesh,
        in_specs=(P("row", "col"), P(), P(("row", "col"), None, None), P(), P("col")),
        out_specs=(P("row", "col"), P("col"), P("col")),
        check_vma=False,
    )
```

```python
import functools

import jax
import jax.numpy as jnp
from jax import lax
from jax.experimental import pallas as pl
from jax.experimental.pallas import tpu as pltpu
from jax.sharding import PartitionSpec as P

I32 = jnp.int32
F32 = jnp.float32
BF = jnp.bfloat16
F8 = jnp.float8_e4m3fn
LANES = 128
BLOCKS = 8192
MESH = pl.DeviceIdType.MESH


def start_gather(evm, hi, sms, sem):
    hi[...] = lax.shift_right_logical(evm[...], 7)
    for k in range(len(sms)):
        pltpu.make_async_copy(hi.at[k], sms[k], sem.at[k]).start()


def gather_labels(evm, table, lab, hi, sms, g, sem):
    tiles = evm.shape[0]
    depth = len(sms)
    sub = lax.broadcasted_iota(I32, (LANES, LANES), 0)

    def finish(t, slot):
        for side in (0, 1):
            lanes = evm[t, pl.ds(side, 1), :] & (LANES - 1)
            picked = jnp.where(sub == lanes, g[slot, side].T, 0)
            lab[side, pl.ds(t, 1), :] = jnp.sum(picked, axis=0, keepdims=True)

    def body(u, _):
        for k in range(depth):
            t = depth * u + k
            pltpu.make_async_copy(hi.at[t], sms[k], sem.at[k]).wait()
            finish(jnp.maximum(t - 1, 0), (k + 1) % 2)
            for side in (0, 1):
                for e in range(LANES):
                    g[k % 2, side, pl.ds(e, 1), :] = table[pl.ds(sms[k][side, e], 1), :]
            later = jnp.minimum(t + depth, tiles - 1)
            pltpu.make_async_copy(hi.at[later], sms[k], sem.at[k]).start()
        return 0

    lax.fori_loop(0, tiles // depth, body, 0)
    for k in range(depth):
        pltpu.make_async_copy(hi.at[tiles - 1], sms[k], sem.at[k]).wait()
    finish(tiles - 1, (depth - 1) % 2)


BLOCK = 256
GROUP = 16
SPREAD = 16
NT = (((1,), (1,)), ((), ()))


def place_entries(lab, enc, hot, slots, send, acc, rows_tile, cols_tile, col_devices):
    tiles = lab.shape[1]
    pair = BLOCK // LANES
    row_bits = rows_tile.bit_length() - 1
    col_bits = cols_tile.bit_length() - 1
    for side in (0, 1):
        row, col = lab[side], lab[1 - side]
        enc[side, 0] = ((row >> row_bits) * col_devices + (col >> col_bits)).astype(F32)
        row = (row & (rows_tile - 1)) + 1
        col = col & (cols_tile - 1)
        for k, piece in enumerate((row & -32, col & -32, row & 31, col & 31)):
            enc[side, k + 1] = piece.astype(F32)
    upper = (
        lax.broadcasted_iota(I32, (BLOCK, BLOCK), 0) <= lax.broadcasted_iota(I32, (BLOCK, BLOCK), 1)
    ).astype(F32).astype(BF)
    dev32 = lax.broadcasted_iota(I32, (LANES, BLOCK), 0).astype(F32)
    dev16 = dev32.astype(BF)
    one = jnp.ones((LANES, BLOCK), BF)
    zero = jnp.zeros((LANES, BLOCK), BF)
    tail16 = (lax.broadcasted_iota(I32, (16, BLOCK), 0) + LANES).astype(F32).astype(BF)
    tail_zero = jnp.zeros((16, BLOCK), BF)
    acc[...] = jnp.zeros_like(acc)

    def line(ref, q, kind=BF):
        return jnp.concatenate([ref[pl.ds(q * pair + n, 1), :] for n in range(pair)], 1).astype(kind)

    def rank(side):
        def body(u, base):
            hots = []
            for q in range(GROUP):
                owner = line(enc.at[side, 0], u * GROUP + q)
                hots.append(jnp.where(dev16 == jnp.broadcast_to(owner, dev16.shape), one, zero))
            lanes = pl.ds(pl.multiple_of(u * GROUP * BLOCK, GROUP * BLOCK), GROUP * BLOCK)
            hot[side, :, lanes] = jnp.concatenate(hots, 1)
            within = jnp.dot(jnp.concatenate(hots, 0), upper, preferred_element_type=F32)
            for q in range(GROUP):
                w = within[q * LANES : (q + 1) * LANES]
                running = w + jnp.concatenate([base, base], 1)
                owner = line(enc.at[side, 0], u * GROUP + q, F32)
                here = dev32 == jnp.broadcast_to(owner, dev32.shape)
                slot = jnp.sum(jnp.where(here, running, 0.0), axis=0, keepdims=True) - 1.0
                for n in range(pair):
                    slots[side, pl.ds((u * GROUP + q) * pair + n, 1), :] = slot[:, n * LANES : (n + 1) * LANES]
                base = base + jnp.broadcast_to(w[:, BLOCK - 1 :], base.shape)
            return base

        return body

    def spread(side):
        def body(u, _):
            columns = []
            for q in range(SPREAD):
                at = u * SPREAD + q
                slot = line(slots.at[side], at)
                main = dev16 == jnp.broadcast_to(slot, dev16.shape)
                tail = tail16 == jnp.broadcast_to(slot, tail16.shape)
                pieces = [line(enc.at[side, k], at) for k in range(1, 5)]
                columns.append(
                    jnp.concatenate(
                        [jnp.where(main, jnp.broadcast_to(v, dev16.shape), zero) for v in pieces]
                        + [jnp.where(tail, jnp.broadcast_to(v, tail16.shape), tail_zero) for v in pieces],
                        0,
                    )
                )
            lanes = pl.ds(pl.multiple_of(u * SPREAD * BLOCK, SPREAD * BLOCK), SPREAD * BLOCK)
            acc[...] += lax.dot_general(
                jnp.concatenate(columns, 1), hot[side, :, lanes], NT, preferred_element_type=F32
            )
            return 0

        return body

    base = jnp.zeros((LANES, LANES), F32)
    for side in (0, 1):
        base = lax.fori_loop(0, tiles // (GROUP * pair), rank(side), base)
    for side in (0, 1):
        lax.fori_loop(0, tiles // (SPREAD * pair), spread(side), 0)
    for k in range(2):
        high = acc[k * LANES : (k + 1) * LANES]
        low = acc[(k + 2) * LANES : (k + 3) * LANES]
        send[k] = (high + low).T.astype(I32)
    tail = acc[4 * LANES : 4 * LANES + 32] + acc[4 * LANES + 32 :]
    send[2] = jnp.concatenate([tail, jnp.zeros((LANES - 32, LANES), F32)], 0).T.astype(I32)


def entropy_term(value):
    return value * jnp.log(jnp.maximum(value, 1.0))


def row_code(r, valid, otherwise):
    code = jnp.where(valid, (128 + (r & 127)) << ((r >> 7) & 7), otherwise)
    return code.astype(F32).astype(BF)


def one_hot(v, n):
    wide = v.shape[1]
    ids = lax.broadcasted_iota(I32, (256, wide), 0).astype(F32).astype(BF)
    one = jnp.ones((256, wide), BF)
    zero = jnp.zeros((256, wide), BF)
    out = []
    for b in range(n // 256):
        w = jnp.where((v >> 8) == b, v & 255, -1).astype(F32).astype(BF)
        out.append(jnp.where(ids == jnp.broadcast_to(w, ids.shape), one.astype(F8), zero.astype(F8)))
    return jnp.concatenate(out, 0)


STEP = 16
TABLE_PARTS = 6
FAR_FIRST = ((2, 2), (1, 2), (2, 1), (2, 3), (3, 2), (0, 2), (1, 1), (1, 3), (2, 0), (3, 1), (3, 3), (0, 1), (0, 3), (1, 0), (3, 0), (0, 0))


def ingest_kernel(
    row_n, col_n, early, proposals_in, edges_in, flags_in, table_in, counts_in,
    updated, cost_out, accepted_out,
    table, counts, evm, psm, pvm, near, flags, lab, enc, hot, slots, hi, s0, s1, s2, s3, g, send, recv, tails, acc,
    columns, picked, col_hot, halves, merged, arrived, packed, finals,
    hsem, lsem, tsem, ssem, rsem, essem, ersem, fssem, frsem,
):
    devices = row_n * col_n
    i = lax.axis_index("row")
    j = lax.axis_index("col")
    me = i * col_n + j
    place_of = lax.rem(j, 4) * (col_n // 4) + j // 4
    my_slot = place_of * row_n + i
    my_group = my_slot // STEP
    rows_tile, cols_tile = counts.shape
    props = pvm.shape[1]
    per_row = props // row_n
    home = j // 2
    sms = (s0, s1, s2, s3)
    barrier = pltpu.get_barrier_semaphore()

    pieces = [pl.ds(k * (table.shape[0] // TABLE_PARTS), table.shape[0] // TABLE_PARTS) for k in range(TABLE_PARTS)]
    load_table = [pltpu.make_async_copy(table_in.at[p], table.at[p], tsem.at[k]) for k, p in enumerate(pieces)]
    load_counts = pltpu.make_async_copy(counts_in, counts, lsem.at[1])
    load_edges = pltpu.make_async_copy(edges_in, evm, lsem.at[2])
    others = (
        pltpu.make_async_copy(proposals_in, pvm, lsem.at[3]),
        pltpu.make_async_copy(flags_in, flags, lsem.at[5]),
    )
    load_edges.start()
    load_updated = pltpu.make_async_copy(counts_in, updated, lsem.at[6])
    load_near = pltpu.make_async_copy(near, psm, lsem.at[4])
    for load in load_table:
        load.start()
    for load in others:
        load.start()

    def peer(r, c):
        return lax.rem(i + r, row_n), lax.rem(j + c, col_n)

    def greet(r, _, first=0):
        for c in range(first, col_n):
            pl.semaphore_signal(barrier, inc=1, device_id=peer(r, c), device_id_type=MESH)
        return 0

    greet(0, 0, 1)
    lax.fori_loop(1, row_n, greet, 0)
    load_edges.wait()
    start_gather(evm, hi, sms, hsem)
    for load in others:
        load.wait()
    near[...] = jnp.clip(pvm[...] - i * rows_tile, 0, rows_tile - 1)
    load_near.start()
    for side in (0, 1):
        for h in range(props // LANES):
            line = pvm[side : side + 1, h * LANES : (h + 1) * LANES]
            columns[side, h * LANES : (h + 1) * LANES, :] = jnp.broadcast_to(line, (LANES, LANES)).T
    load_near.wait()
    for load in load_table:
        load.wait()
    load_counts.start()
    load_updated.start()
    gather_labels(evm, table, lab, hi, sms, g, hsem)
    place_entries(lab, enc, hot, slots, send, acc, rows_tile, cols_tile, col_n)
    pl.semaphore_wait(barrier, devices - 1)

    def push(t, _, last=0):
        r = row_n // 2 + (t + 1) // 2 * (2 * lax.rem(t, 2) - 1)
        row = lax.rem(i + r, row_n)
        for dz, dy in FAR_FIRST[: len(FAR_FIRST) - last]:
            col = lax.rem(j // 4 + dz, 4) * 4 + lax.rem(j + dy, 4)
            pltpu.make_async_remote_copy(
                src_ref=send.at[:, pl.ds(row * col_n + col, 1), :],
                dst_ref=recv.at[:, pl.ds(my_slot, 1), :],
                send_sem=ssem,
                recv_sem=rsem.at[my_group],
                device_id=(row, col),
                device_id_type=MESH,
            ).start()
        return 0

    lax.fori_loop(0, row_n - 1, push, 0)
    push(row_n - 1, 0, 1)
    recv[:, pl.ds(my_slot, 1), :] = send[:, pl.ds(me, 1), :]
    load_counts.wait()

    def pick(u, _):
        block = picked.at[pl.ds(pl.multiple_of(u * 8, 8), 8), :]
        for q in range(8):
            block[q : q + 1, :] = counts[pl.ds(psm[1, u * 8 + q], 1), :]
        return 0

    lax.fori_loop(0, props // 8, pick, 0)
    for q in range(per_row):
        picked[props + q : props + q + 1, :] = counts[pl.ds(psm[0, i * per_row + q], 1), :]
    apart = columns[1] - i * rows_tile
    inside = jnp.logical_and(apart >= 0, apart < rows_tile)
    picked[:props, :] = jnp.where(
        jnp.concatenate([inside] * (cols_tile // LANES), 1), picked[:props, :], 0.0
    )

    mine = pl.ds(pl.multiple_of(i * per_row, 8), per_row)
    source = columns[0, mine, :]
    target = columns[1, mine, :]
    wanted = jnp.concatenate([columns[1], source], 0) - i * rows_tile
    wanted = row_code(wanted, jnp.logical_and(wanted >= 0, wanted < rows_tile), -1)

    def lanes_of(ref, s):
        return jnp.concatenate([ref[pl.ds(s * STEP + q, 1), :] for q in range(STEP)], 1)

    def small(s, rows, cols):
        hot = one_hot(cols, cols_tile)
        col_hot[s] = hot
        code = row_code(rows, rows >= 0, 0)
        tall = jnp.concatenate([wanted] * STEP, 1)
        match = jnp.where(
            tall == jnp.broadcast_to(code, tall.shape), jnp.ones(tall.shape, BF), jnp.zeros(tall.shape, BF)
        ).astype(F8)
        picked[...] += lax.dot_general(match, hot, NT, preferred_element_type=F32)

    groups = devices // STEP

    def arrive(s, _):
        @pl.when(s == my_group)
        def _():
            part = recv.at[:, pl.ds(0, STEP - 1), :]
            pltpu.make_async_copy(part, part, rsem.at[s]).wait()

        @pl.when(s != my_group)
        def _():
            part = recv.at[:, pl.ds(0, STEP), :]
            pltpu.make_async_copy(part, part, rsem.at[s]).wait()

        small(s, lanes_of(recv.at[0], s) - 1, lanes_of(recv.at[1], s))
        return 0

    lax.fori_loop(0, groups, arrive, 0)
    tails[...] = recv[2].T
    last_rows = jnp.concatenate([tails[q : q + 1] for q in range(16)], 1) - 1
    last_cols = jnp.concatenate([tails[q : q + 1] for q in range(16, 32)], 1)
    small(groups, last_rows, last_cols)

    x = i // 2
    core = lax.rem(i, 2)
    chips = row_n // 2

    def chunk(k, c):
        return pl.ds(pl.multiple_of((lax.rem(x + k, chips) * 2 + c) * per_row, 8), per_row)

    def first(k):
        return pltpu.make_async_remote_copy(
            src_ref=picked.at[chunk(k, 1 - core), :],
            dst_ref=halves.at[k],
            send_sem=essem.at[k],
            recv_sem=ersem.at[k],
            device_id=(x * 2 + 1 - core, j),
            device_id_type=MESH,
        )

    def second(k):
        return pltpu.make_async_remote_copy(
            src_ref=merged.at[k],
            dst_ref=arrived.at[k],
            send_sem=essem.at[chips + k],
            recv_sem=ersem.at[chips + k],
            device_id=(lax.rem(x + k, chips) * 2 + core, j),
            device_id_type=MESH,
        )

    far_first = (2, 1, 3, 0)
    for k in far_first:
        first(k).start()

    def add(s, rows):
        updated[...] += lax.dot_general(
            one_hot(rows, rows_tile), col_hot[s], NT, preferred_element_type=F32
        )

    def add_step(s, _):
        add(s, lanes_of(recv.at[0], s) - 1)
        return 0

    load_updated.wait()
    lax.fori_loop(0, 1, add_step, 0)
    for k in far_first:
        first(k).wait_recv()
        merged[k] = picked[chunk(k, core), :] + halves[k]
        if k > 0:
            second(k).start()
    lax.fori_loop(1, early, add_step, 0)
    rest = pl.ds(0, devices - 1)
    pltpu.make_async_copy(send.at[:, rest, :], send.at[:, rest, :], ssem).wait()

    other = merged[0]
    for k in range(chips):
        first(k).wait_send()
        if k > 0:
            second(k).wait()
            other += arrived[k]
    own = picked[props:, :]
    where_at = lax.broadcasted_iota(I32, own.shape, 1) + j * cols_tile
    wide4 = cols_tile // LANES
    at_source = where_at == jnp.concatenate([source] * wide4, 1)
    at_target = where_at == jnp.concatenate([target] * wide4, 1)
    mixed = entropy_term(own + other) - entropy_term(own) - entropy_term(other)
    parts = (
        jnp.where(jnp.logical_or(at_source, at_target), 0.0, mixed),
        jnp.where(at_source, own, 0.0),
        jnp.where(at_source, other, 0.0),
        jnp.where(at_target, other, 0.0),
        own,
        other,
    )
    half = per_row // 2
    lane = lax.broadcasted_iota(I32, (per_row, LANES), 1)
    table6 = jnp.zeros((per_row, LANES), F32)
    for k, part in enumerate(parts):
        table6 = jnp.where((lane >> (half.bit_length() - 1)) == k, jnp.sum(part, axis=1, keepdims=True), table6)
    row = lax.broadcasted_iota(I32, (per_row, LANES), 0)
    table6 = jnp.where((lane & (half - 1)) == (row & (half - 1)), table6, 0.0)
    for h in range(2):
        packed[h] = jnp.sum(table6[h * half : (h + 1) * half], axis=0, keepdims=True)

    for k in range(2 * row_n):
        d = (k // 2, 2 * i + k % 2)
        same = jnp.logical_and(d[0] == i, d[1] == j)

        @pl.when(jnp.logical_not(same))
        def _():
            pltpu.make_async_remote_copy(
                src_ref=packed.at[k % 2], dst_ref=finals.at[j], send_sem=fssem, recv_sem=frsem,
                device_id=d, device_id_type=MESH,
            ).start()

    @pl.when(home == i)
    def _():
        finals[j] = packed[lax.rem(j, 2)]

    lax.fori_loop(early, groups, add_step, 0)
    add(groups, jnp.concatenate([tails[q : q + 1] for q in range(16)], 1) - 1)

    @pl.when(home == i)
    def _():
        fewer = pl.ds(0, col_n - 1)
        pltpu.make_async_copy(finals.at[fewer], finals.at[fewer], fssem).wait()
        pltpu.make_async_copy(finals.at[fewer], finals.at[fewer], frsem).wait()

    @pl.when(home != i)
    def _():
        pltpu.make_async_copy(finals, finals, fssem).wait()
        pltpu.make_async_copy(finals, finals, frsem).wait()

    sums = jnp.sum(finals[...], axis=0)
    per_col = props // col_n
    pair, self_source, cross, self_target, degree_source, degree_target = [
        sums[:, k * per_col : (k + 1) * per_col] for k in range(6)
    ]
    corner = (
        entropy_term(self_source + 2.0 * cross + self_target)
        - entropy_term(self_source)
        - entropy_term(self_target)
        - 2.0 * entropy_term(cross)
    )
    change = (
        -(pair + 0.5 * corner)
        + entropy_term(degree_source + degree_target)
        - entropy_term(degree_source)
        - entropy_term(degree_target)
    )
    cost = change / BLOCKS
    cost_out[...] = cost
    accepted_out[...] = jnp.where(flags[...] == 1, cost, 0.0)


def ingest(proposals, edge_tiles, flags, labels, counts, row_n, col_n):
    props = proposals.shape[1]
    per_row = props // row_n
    rows_tile, cols_tile = counts.shape
    tiles = edge_tiles.shape[0]
    devices = row_n * col_n
    table = labels.reshape(-1, LANES)
    vm = pl.BlockSpec(memory_space=pltpu.VMEM)
    anywhere = pl.BlockSpec(memory_space=pltpu.HBM)
    small = pltpu.SMEM((2, LANES), I32)
    dma = pltpu.SemaphoreType.DMA
    out16 = pltpu.VMEM(flags.shape, F32)
    return pl.pallas_call(
        functools.partial(ingest_kernel, row_n, col_n, 4),
        out_shape=(pltpu.VMEM(counts.shape, F32), out16, out16),
        in_specs=[anywhere] * 5,
        out_specs=(vm, vm, vm),
        scratch_shapes=[
            pltpu.VMEM(table.shape, I32),
            pltpu.VMEM(counts.shape, F32),
            pltpu.VMEM(edge_tiles.shape, I32),
            pltpu.SMEM(proposals.shape, I32),
            pltpu.VMEM(proposals.shape, I32),
            pltpu.VMEM(proposals.shape, I32),
            pltpu.VMEM(flags.shape, I32),
            pltpu.VMEM((2, tiles, LANES), I32),
            pltpu.VMEM((2, 5, tiles, LANES), F32),
            pltpu.VMEM((2, LANES, tiles * LANES), BF),
            pltpu.VMEM((2, tiles, LANES), F32),
            pltpu.VMEM(edge_tiles.shape, I32),
            small,
            small,
            small,
            small,
            pltpu.VMEM((2, 2, LANES, LANES), I32),
            pltpu.VMEM((3, devices, LANES), I32),
            pltpu.VMEM((3, devices, LANES), I32),
            pltpu.VMEM((LANES, LANES), I32),
            pltpu.VMEM((576, LANES), F32),
            pltpu.VMEM((2, props, LANES), I32),
            pltpu.VMEM((props + per_row, cols_tile), F32),
            pltpu.VMEM((devices // STEP + 1, cols_tile, STEP * LANES), F8),
            pltpu.VMEM((row_n // 2, per_row, cols_tile), F32),
            pltpu.VMEM((row_n // 2, per_row, cols_tile), F32),
            pltpu.VMEM((row_n // 2, per_row, cols_tile), F32),
            pltpu.VMEM((2, 1, LANES), F32),
            pltpu.VMEM((col_n, 1, LANES), F32),
            dma((4,)),
            dma((7,)),
            dma((TABLE_PARTS,)),
            dma,
            dma((devices // STEP,)),
            dma((row_n,)),
            dma((row_n,)),
            dma,
            dma,
        ],
        compiler_params=pltpu.CompilerParams(
            collective_id=0,
            has_side_effects=True,
            vmem_limit_bytes=32 << 20,
        ),
    )(*[
        pltpu.with_memory_space_constraint(x, pltpu.HBM)
        for x in (proposals, edge_tiles, flags, table, counts)
    ])


def finish_kernel(updated_in, cost_in, accepted_in, updated, cost, accepted, sem):
    copy = pltpu.make_async_copy(updated_in, updated, sem)
    copy.start()
    cost[...] = cost_in[...]
    accepted[...] = accepted_in[...]
    copy.wait()


def per_device(counts, labels, edge_tiles, proposals, accept_flags):
    row_n = lax.axis_size("row")
    col_n = lax.axis_size("col")
    flags = accept_flags.reshape(1, -1)
    parts = ingest(proposals, edge_tiles, flags, labels, counts, row_n, col_n)
    vm = pl.BlockSpec(memory_space=pltpu.VMEM)
    out16 = jax.ShapeDtypeStruct(flags.shape, F32)
    updated, cost, accepted = pl.pallas_call(
        finish_kernel,
        out_shape=(jax.ShapeDtypeStruct(counts.shape, F32), out16, out16),
        in_specs=[vm] * 3,
        out_specs=(pl.BlockSpec(memory_space=pltpu.HBM), vm, vm),
        scratch_shapes=[pltpu.SemaphoreType.DMA],
        compiler_params=pltpu.CompilerParams(vmem_limit_bytes=8 << 20),
    )(*parts)
    return updated, cost.reshape(-1), accepted.reshape(-1)


def solution(mesh):
    return jax.shard_map(
        per_device,
        mesh=mesh,
        in_specs=(P("row", "col"), P(), P(("row", "col"), None, None), P(), P("col")),
        out_specs=(P("row", "col"), P("col"), P("col")),
        check_vma=False,
    )
```
